128 devices in a mesh: row: 16 (over x_lo, z, core), col: 8 (over y, x_hi).
Axes of the slice: x: 4 (x_hi: 2, x_lo: 2; x = x_hi * 2 + x_lo), y: 4, z: 4, core: 2. Of those that a mesh axis runs over, the one named last changes fastest.
Arguments:
- new_velocity: float32 [3, 160, 160, 160], P(None, 'row', 'col'), may hold values from -6 to 6
- stored_velocity: float32 [6, 3, 256, 256, 256], P(None, None, 'row', 'col'), may hold values from -6 to 6
- stored_vorticity: float32 [6, 3, 256, 256, 256], P(None, None, 'row', 'col'), may hold values from -6 to 6
Outputs:
- next_velocity: float32 [3, 160, 160, 160], P(None, 'row', 'col')
The draws below stay inside these ranges and needn't reach their ends.
All inputs are finite; a program needn't handle non-finite values.
Results may differ from the reference program's by a relative error of at most 0.00007.
Values sent between devices are 32-bit elements; how exact they have to be, the bound alone decides.
A program may use at most 128 MiB of HBM per device.

```python
import math
import jax
import jax.numpy as jnp
from jax import lax

N = 256
MODES = 160
ORDERS = 6
KMAX = 79


def shard_levels(key, dims, split, least, high):
    level = 1.0
    for dim, blocks in split:
        heights = jax.random.uniform(jax.random.fold_in(jax.random.fold_in(key, 6), dim), (blocks,), jnp.float32, least / len(split), high / len(split))
        level = level * jnp.repeat(jnp.exp(heights), dims[dim] // blocks).reshape((-1,) + (1,) * (len(dims) - 1 - dim))
    return level


def normal_values(key, dims, spread, bound, cuts=(), held_as=jnp.bfloat16):
    level = shard_levels(key, dims, cuts, -0.22, 0.18) if cuts else 1.0
    array = jax.random.normal(key, dims, jnp.float32) * spread * level
    return jnp.minimum(jnp.maximum(array, -bound), bound).astype(held_as)


def setup_inputs(seed: int = 0) -> dict:
    seeds = jax.random.split(jax.random.key(seed), 4)
    return {
        "new_velocity": normal_values(seeds[0], (3, MODES, MODES, MODES), 1.0, 6.0, ((1, 16), (2, 8)), jnp.float32),
        "stored_velocity": normal_values(seeds[1], (ORDERS, 3, N, N, N), 1.0, 6.0, ((2, 16), (3, 8)), jnp.float32),
        "stored_vorticity": normal_values(seeds[2], (ORDERS, 3, N, N, N), 1.0, 6.0, ((2, 16), (3, 8)), jnp.float32),
    }


highest = lax.Precision.HIGHEST

def synth_table(grid_len, mode_count):
    points = jnp.arange(grid_len, dtype=jnp.int32)[:, None]
    mode_index = jnp.arange(mode_count, dtype=jnp.int32)[None, :]
    wave_index = jnp.where(mode_index == 1, grid_len // 2, mode_index // 2)
    angles = (points * wave_index % grid_len).astype(jnp.float32) * (2.0 * math.pi / grid_len)
    trig_values = jnp.where((mode_index % 2 == 0) | (mode_index == 1), jnp.cos(angles), jnp.sin(angles))
    weight = jnp.where(mode_index < 2, 1.0, 2.0).astype(jnp.float32) / grid_len
    return trig_values * jnp.sqrt(weight)

def keep_modes(mode_index):
    return (mode_index != 1).astype(jnp.float32)

def pair_slope(spectra, axis_pos, wavenum):
    full_shape = spectra.shape
    half_len = full_shape[axis_pos] // 2
    paired = spectra.reshape(full_shape[:axis_pos] + (half_len, 2) + full_shape[axis_pos + 1:])
    pair_view = [1] * (len(full_shape) + 1)
    pair_view[axis_pos] = half_len
    scaled = wavenum.reshape(tuple(pair_view))
    even_part = lax.slice_in_dim(paired, 0, 1, axis=axis_pos + 1)
    odd_part = lax.slice_in_dim(paired, 1, 2, axis=axis_pos + 1)
    return jnp.concatenate([scaled * odd_part, -scaled * even_part], axis=axis_pos + 1).reshape(full_shape)

def synth_three(spectra, basis_table):
    section_one = jnp.einsum('yzm,xm->xyz', spectra, basis_table, precision=highest)
    section_two = jnp.einsum('xmz,ym->xyz', section_one, basis_table, precision=highest)
    return jnp.einsum('xym,zm->xyz', section_two, basis_table, precision=highest)

def analyze_three(physical, basis_table):
    section_one = jnp.einsum('xyz,zc->xyc', physical, basis_table, precision=highest)
    section_two = jnp.einsum('xyc,yk->xkc', section_one, basis_table, precision=highest)
    return jnp.einsum('xkc,xj->kcj', section_two, basis_table, precision=highest)

def cross_prod(left, right):
    return jnp.stack([left[1] * right[2] - left[2] * right[1], left[2] * right[0] - left[0] * right[2], left[0] * right[1] - left[1] * right[0]])

def reference(new_velocity, stored_velocity, stored_vorticity):
    mode_index = jnp.arange(MODES, dtype=jnp.int32)
    keep_flag = keep_modes(mode_index)
    wavenum = (mode_index[0::2] // 2).astype(jnp.float32) / KMAX
    keep_mask = keep_flag[:, None, None] * keep_flag[None, :, None] * keep_flag[None, None, :]
    coeffs = new_velocity * keep_mask
    coef_x, coef_y, coef_z = (coeffs[0], coeffs[1], coeffs[2])
    vort_x = pair_slope(coef_z, 0, wavenum) - pair_slope(coef_y, 1, wavenum)
    vort_y = pair_slope(coef_x, 1, wavenum) - pair_slope(coef_z, 2, wavenum)
    vort_z = pair_slope(coef_y, 2, wavenum) - pair_slope(coef_x, 0, wavenum)
    basis_table = synth_table(N, MODES)
    velocity_new = jnp.stack([synth_three(coef_x, basis_table), synth_three(coef_y, basis_table), synth_three(coef_z, basis_table)])
    vorticity_new = jnp.stack([synth_three(vort_x, basis_table), synth_three(vort_y, basis_table), synth_three(vort_z, basis_table)])
    cauchy_sum = cross_prod(velocity_new, stored_vorticity[0]) + cross_prod(stored_velocity[0], vorticity_new)
    for order_idx in range(1, ORDERS):
        cauchy_sum = cauchy_sum + cross_prod(stored_velocity[order_idx], stored_vorticity[ORDERS - order_idx])
    spectral = jnp.stack([analyze_three(cauchy_sum[0], basis_table), analyze_three(cauchy_sum[1], basis_table), analyze_three(cauchy_sum[2], basis_table)]) * keep_mask
    wave_mode = (mode_index // 2).astype(jnp.float32) / KMAX
    wave_square = wave_mode[:, None, None] ** 2 + wave_mode[None, :, None] ** 2 + wave_mode[None, None, :] ** 2
    divergence = pair_slope(spectral[0], 2, wavenum) + pair_slope(spectral[1], 0, wavenum) + pair_slope(spectral[2], 1, wavenum)
    potential = jnp.where(wave_square > 0, divergence / jnp.where(wave_square > 0, wave_square, 1.0), 0.0)
    result = jnp.stack([spectral[0] + pair_slope(potential, 2, wavenum), spectral[1] + pair_slope(potential, 0, wavenum), spectral[2] + pair_slope(potential, 1, wavenum)])
    return result / (ORDERS + 1)
```

```python
import jax
import jax.numpy as jnp
import numpy as np
from jax import lax
from jax.experimental import pallas as pl
from jax.experimental.pallas import tpu as pltpu
from jax.sharding import PartitionSpec as P

N = 256
MODES = 160
ORDERS = 6
KMAX = 79
ROWS, COLS = 16, 8
KY, KZ = MODES // ROWS, MODES // COLS
XL, YL = N // ROWS, N // COLS
CHUNKS = 4
XC = XL // CHUNKS
XP = XC // 2
OFFSETS = (0, 20, 40, 64, 84, 104)
MESH = pl.DeviceIdType.MESH
bf16, f32 = jnp.bfloat16, jnp.float32


def basis():
    p = np.arange(N)[:, None]
    m = np.arange(MODES)[None, :]
    k = m // 2
    angle = 2.0 * np.pi / N * (p * k % N)
    table = np.where(m % 2 == 0, np.cos(angle), np.sin(angle)) * np.sqrt(np.where(m < 2, 1.0, 2.0) / N)
    table[:, 1] = 0.0
    return table


def halves(table):
    high = np.asarray(table, jnp.bfloat16)
    low = np.asarray(table - high.astype(np.float64), jnp.bfloat16)
    return high, low


def tables():
    s = basis()
    sx = np.zeros((N, 256))
    sx[:, :MODES] = s
    order = np.arange(MODES).reshape(ROWS, KY).T.reshape(-1)
    sy_h, sy_l = halves(s[:, order])
    sy = np.concatenate([sy_h, sy_h, sy_l, np.zeros((N, 32), jnp.bfloat16)], axis=1)
    sz = np.zeros((256, N))
    sz[:120] = s[:, :120].T
    sz[128:168] = s[:, 120:].T
    ya = np.concatenate([sy_h.T, sy_h.T, sy_l.T], axis=1)
    points = np.arange(N).reshape(ROWS, XL // 2, 2).transpose(2, 0, 1).reshape(-1)
    xa = np.zeros((N, 256))
    xa[:, :MODES] = s[points]
    return (*halves(sx), sy, *halves(sz), *halves(sz.T), ya, *halves(xa))


def split(x):
    high = x.astype(bf16)
    return high, (x - high.astype(f32)).astype(bf16)


def dot(a, b):
    return jnp.dot(a, b, preferred_element_type=f32)


def dot_nt(a, b):
    return lax.dot_general(a, b, (((1,), (1,)), ((), ())), preferred_element_type=f32)


def dot3(x, table_h, table_l):
    high, low = split(x)
    return dot(high, table_h[...]) + (dot(low, table_h[...]) + dot(high, table_l[...]))


def roll(x, shift, axis):
    shift %= x.shape[axis]
    return x if shift == 0 else pltpu.roll(x, shift, axis)


def pair_swap(x, axis):
    even = lax.broadcasted_iota(jnp.int32, x.shape, axis) % 2 == 0
    return jnp.where(even, roll(x, -1, axis), -roll(x, 1, axis))


def kernel(
    a_ref, vel_hbm, vort_hbm, sxh, sxl, sy, szh, szl, zah, zal, ya, xah, xal,
    out_ref,
    a_s, f_s, vel, vort, part, send1, recv1, send2, recv2, send3, recv3, send4, recv4, fin,
    hbm_sem, s1s, s1r, s2s, s2r, s3s, s3r, s4s, s4r, own,
):
    r, c = lax.axis_index("row"), lax.axis_index("col")

    def row_peer(i):
        return lax.rem(r + i, ROWS)

    def col_peer(i):
        return lax.rem(c + i, COLS)

    barrier = pltpu.get_barrier_semaphore()
    for i in range(1, ROWS):
        pl.semaphore_signal(barrier, 1, device_id=(row_peer(i), c), device_id_type=MESH)
    for i in range(1, COLS):
        pl.semaphore_signal(barrier, 1, device_id=(r, col_peer(i)), device_id_type=MESH)

    def stored(o):
        return (
            pltpu.make_async_copy(vel_hbm.at[o], vel.at[o], hbm_sem.at[0, o]),
            pltpu.make_async_copy(vort_hbm.at[o], vort.at[o], hbm_sem.at[1, o]),
        )

    for o in (1, 5, 2, 4, 3, 0):
        for copy in stored(o):
            copy.start()

    def ds(start, size, unit):
        return pl.ds(pl.multiple_of(start, unit), size)

    def copy1(h, i):
        there = row_peer(i)
        return pltpu.make_async_remote_copy(
            send1.at[:, ds(there * XL + 8 * h, 8, 8), :],
            recv1.at[:, ds(r * XL + 8 * h, 8, 8), :],
            s1s.at[h, i], s1r.at[h, i], device_id=(there, c), device_id_type=MESH,
        )

    def copy2(g, i):
        there = col_peer(i)
        return pltpu.make_async_remote_copy(
            send2.at[pl.ds(g * XC, XC), ds(there * YL, YL, 8), :],
            recv2.at[c, pl.ds(g * XC, XC)],
            s2s.at[g, i], s2r.at[g, i], device_id=(r, there), device_id_type=MESH,
        )

    def copy3(g, i):
        there = col_peer(i)
        return pltpu.make_async_remote_copy(
            send3.at[there, pl.ds(g * XP, XP)],
            recv3.at[pl.ds(g * XP, XP), ds(c * YL, YL, 8), :],
            s3s.at[g, i], s3r.at[g, i], device_id=(r, there), device_id_type=MESH,
        )

    def copy4(i):
        there = row_peer(i)
        return pltpu.make_async_remote_copy(
            send4.at[:, ds(there * 8, 8, 8), :],
            recv4.at[:, ds(r * 8, 8, 8), :],
            s4s.at[i], s4r.at[i], device_id=(there, c), device_id_type=MESH,
        )

    own1 = pltpu.make_async_copy(send1.at[:, ds(r * XL, XL, 8), :], recv1.at[:, ds(r * XL, XL, 8), :], own.at[0])
    own4 = pltpu.make_async_copy(send4.at[:, ds(r * 8, 8, 8), :], recv4.at[:, ds(r * 8, 8, 8), :], own.at[1])

    def own2(g):
        return pltpu.make_async_copy(
            send2.at[pl.ds(g * XC, XC), ds(c * YL, YL, 8), :], recv2.at[c, pl.ds(g * XC, XC)], own.at[2 + g]
        )

    def own3(g):
        return pltpu.make_async_copy(
            send3.at[c, pl.ds(g * XP, XP)], recv3.at[pl.ds(g * XP, XP), ds(c * YL, YL, 8), :], own.at[2 + CHUNKS + g]
        )

    lane = lax.broadcasted_iota(jnp.int32, (24, 256), 1)
    sub = lax.broadcasted_iota(jnp.int32, (24, 256), 0)
    wave_x = (lane // 2).astype(f32) / KMAX
    wave_z = (sub // 2 + c * (KZ // 2)).astype(f32) / KMAX

    def wave_y(pair):
        return (jnp.zeros((24, 256), jnp.int32) + (r * (KY // 2) + pair)).astype(f32) / KMAX

    def diff_x(v):
        return wave_x * pair_swap(v, 1)

    def diff_z(v):
        return wave_z * pair_swap(v, 0)

    a_s[...] = jnp.zeros_like(a_s)
    f_s[...] = jnp.zeros_like(f_s)

    def fields(pair, carry):
        wy = wave_y(pair)
        for k in range(2):
            for i in range(3):
                a_s[k, i, 0:KZ, 0:MODES] = a_ref[i, 2 * pair + k]
        for k in range(2):
            v = [a_s[k, i] for i in range(3)]
            wy_k = wy if k == 0 else -wy
            dy = [wy_k * a_s[1 - k, i] for i in range(3)]
            v += [dy[2] - diff_z(v[1]), diff_z(v[0]) - diff_x(v[2]), diff_x(v[1]) - dy[0]]
            for i in range(6):
                f_s[128 * k + KZ * i : 128 * k + KZ * (i + 1), :] = v[i][0:KZ]
        high, low = split(f_s[...])
        o = dot_nt(sxh[...], high) + (dot_nt(sxh[...], low) + dot_nt(sxl[...], high))
        send1[2 * pair] = o[:, :128]
        send1[2 * pair + 1] = o[:, 128:]
        return carry

    lax.fori_loop(0, KY // 2, fields, 0)

    own1.start()
    pl.semaphore_wait(barrier, ROWS + COLS - 2)
    for h in range(2):
        for i in range(1, ROWS):
            copy1(h, i).start()

    for o in (1, 5, 2, 4, 3):
        for copy in stored(o):
            copy.wait()

    def old_terms(x, carry):
        acc = None
        for o in range(1, ORDERS):
            u = [vel[o, i, x] for i in range(3)]
            w = [vort[ORDERS - o, i, x] for i in range(3)]
            term = [u[1] * w[2] - u[2] * w[1], u[2] * w[0] - u[0] * w[2], u[0] * w[1] - u[1] * w[0]]
            acc = term if acc is None else [p + q for p, q in zip(acc, term)]
        for i in range(3):
            part[i, x] = acc[i]
        return carry

    lax.fori_loop(0, XL, old_terms, 0)
    for copy in stored(0):
        copy.wait()

    def synth_y(xp, carry):
        t = []
        for k in range(2):
            rows = pl.ds(2 * xp + k, ROWS, stride=XL)
            t.append(jnp.concatenate([recv1[m, rows, :] for m in range(KY)], axis=0))
        high, low = split(jnp.concatenate(t, axis=1))
        rhs = jnp.concatenate([high, low, high, jnp.zeros((32, 256), bf16)], axis=0)
        o = dot(sy[...], rhs)
        send2[2 * xp] = o[:, :128]
        send2[2 * xp + 1] = o[:, 128:]
        return carry

    own1.wait()
    for h in range(2):
        for i in range(1, ROWS):
            copy1(h, i).wait_recv()
        for g in range(h * CHUNKS // 2, (h + 1) * CHUNKS // 2):
            lax.fori_loop(g * XP, (g + 1) * XP, synth_y, 0)
            own2(g).start()
            for i in range(1, COLS):
                copy2(g, i).start()

    lane_y = lax.broadcasted_iota(jnp.int32, (YL, 128), 1)

    def place(first):
        q = lane_y - first
        return jnp.where(q < 0, q + 128, q)

    def middle(xp, carry):
        sums = []
        for k in range(2):
            x = 2 * xp + k
            blocks = [roll(recv2[m, x], KZ * (m % 6), 1) for m in range(COLS)]
            tile1, tile2 = [], []
            for i in range(6):
                q = place(KZ * i)
                t = blocks[0]
                for m in range(1, 6):
                    t = jnp.where(q >= KZ * m, blocks[m], t)
                tile1.append(roll(t, -KZ * i, 1))
                tile2.append(roll(jnp.where(q >= KZ, blocks[7], blocks[6]), -KZ * i, 1))
            modes = jnp.concatenate([jnp.concatenate(tile1, axis=0), jnp.concatenate(tile2, axis=0)], axis=1)
            new = dot3(modes, szh, szl)
            u = [new[YL * i : YL * (i + 1)] for i in range(3)]
            w = [new[YL * i : YL * (i + 1)] for i in range(3, 6)]
            v0 = [vel[0, i, x] for i in range(3)]
            w0 = [vort[0, i, x] for i in range(3)]
            for i in range(3):
                a, b = (i + 1) % 3, (i + 2) % 3
                sums.append(part[i, x] + ((u[a] * w0[b] - u[b] * w0[a]) + (v0[a] * w[b] - v0[b] * w[a])))
        o = dot3(jnp.concatenate(sums, axis=0), zah, zal)
        out = [o[YL * j : YL * (j + 1)] for j in range(6)]
        for half in range(2):
            rolled = [roll(out[j][:, 128 * half : 128 * half + 128], OFFSETS[j], 1) for j in range(6)]
            for m in range(6 if half == 0 else 2):
                q = place(KZ * m)
                t = rolled[0]
                for j in range(1, 6):
                    t = jnp.where(q >= OFFSETS[j], rolled[j], t)
                send3[6 * half + m, xp] = roll(t, -KZ * m, 1)
        return carry

    for g in range(CHUNKS):
        own2(g).wait()
        for i in range(1, COLS):
            copy2(g, i).wait_recv()
        lax.fori_loop(g * XP, (g + 1) * XP, middle, 0)
        own3(g).start()
        for i in range(1, COLS):
            copy3(g, i).start()

    def analyze_y(xq, carry):
        high, low = split(jnp.concatenate([recv3[2 * xq], recv3[2 * xq + 1]], axis=1))
        o = dot(ya[...], jnp.concatenate([high, low, high], axis=0))
        for k in range(2):
            for m in range(KY):
                send4[m, pl.ds(2 * xq + k, ROWS, stride=8), :] = o[ROWS * m : ROWS * (m + 1), 128 * k : 128 * k + 128]
        return carry

    for g in range(CHUNKS):
        own3(g).wait()
        for i in range(1, COLS):
            copy3(g, i).wait_recv()
        lax.fori_loop(g * XP // 2, (g + 1) * XP // 2, analyze_y, 0)
    own4.start()
    for i in range(1, ROWS):
        copy4(i).start()
    own4.wait()
    for i in range(1, ROWS):
        copy4(i).wait_recv()

    def finish(pair, carry):
        rows = []
        for k in range(2):
            t = recv4[2 * pair + k].T
            rows.append(jnp.concatenate([t[0:64], t[64:128]], axis=1))
        fin[...] = dot3(jnp.concatenate(rows, axis=0), xah, xal)
        s = [[fin[64 * k + KZ * i : 64 * k + KZ * i + 24, :] for i in range(3)] for k in range(2)]
        wy = wave_y(pair)
        square = wave_y(pair) ** 2 + wave_z**2 + wave_x**2
        some = square > 0
        safe = jnp.where(some, square, 1.0)
        potential = []
        for k in range(2):
            wy_k = wy if k == 0 else -wy
            divergence = diff_x(s[k][0]) + wy_k * s[1 - k][1] + diff_z(s[k][2])
            potential.append(jnp.where(some, divergence / safe, 0.0))
        for k in range(2):
            wy_k = wy if k == 0 else -wy
            slopes = (diff_x(potential[k]), wy_k * potential[1 - k], diff_z(potential[k]))
            for i in range(3):
                out_ref[i, 2 * pair + k] = ((s[k][i] + slopes[i]) / (ORDERS + 1))[0:KZ, 0:MODES]
        return carry

    lax.fori_loop(0, KY // 2, finish, 0)

    for i in range(1, ROWS):
        copy1(0, i).wait_send()
        copy1(1, i).wait_send()
        copy4(i).wait_send()
    for g in range(CHUNKS):
        for i in range(1, COLS):
            copy2(g, i).wait_send()
            copy3(g, i).wait_send()


def shards(new_velocity, stored_velocity, stored_vorticity):
    consts = tables()
    vmem = pl.BlockSpec(memory_space=pltpu.VMEM)
    hbm = pl.BlockSpec(memory_space=pl.ANY)
    dma = pltpu.SemaphoreType.DMA
    return pl.pallas_call(
        kernel,
        out_shape=jax.ShapeDtypeStruct((3, KY, KZ, MODES), f32),
        in_specs=[vmem, hbm, hbm] + [vmem] * len(consts),
        out_specs=vmem,
        scratch_shapes=[
            pltpu.VMEM((2, 3, 24, 256), f32),
            pltpu.VMEM((256, 256), f32),
            pltpu.VMEM((ORDERS, 3, XL, YL, N), f32),
            pltpu.VMEM((ORDERS, 3, XL, YL, N), f32),
            pltpu.VMEM((3, XL, YL, N), f32),
            pltpu.VMEM((KY, N, 128), f32),
            pltpu.VMEM((KY, N, 128), f32),
            pltpu.VMEM((XL, N, 128), f32),
            pltpu.VMEM((COLS, XL, YL, 128), f32),
            pltpu.VMEM((COLS, XL // 2, YL, 128), f32),
            pltpu.VMEM((XL // 2, N, 128), f32),
            pltpu.VMEM((KY, 128, 128), f32),
            pltpu.VMEM((KY, 128, 128), f32),
            pltpu.VMEM((128, 256), f32),
            dma((2, ORDERS)),
            dma((2, ROWS)),
            dma((2, ROWS)),
            dma((CHUNKS, COLS)),
            dma((CHUNKS, COLS)),
            dma((CHUNKS, COLS)),
            dma((CHUNKS, COLS)),
            dma((ROWS,)),
            dma((ROWS,)),
            dma((2 + 2 * CHUNKS,)),
        ],
        compiler_params=pltpu.CompilerParams(
            collective_id=0, has_side_effects=True, vmem_limit_bytes=60 * 2**20
        ),
        name="euler_order",
    )(new_velocity, stored_velocity, stored_vorticity, *map(jnp.asarray, consts))


def solution(mesh):
    return jax.shard_map(
        shards,
        mesh=mesh,
        in_specs=(
            P(None, "row", "col", None),
            P(None, None, "row", "col", None),
            P(None, None, "row", "col", None),
        ),
        out_specs=P(None, "row", "col", None),
        check_vma=False,
    )
```

```python
import jax
import jax.numpy as jnp
import numpy as np
from jax import lax
from jax.experimental import pallas as pl
from jax.experimental.pallas import tpu as pltpu
from jax.sharding import PartitionSpec as P

N = 256
MODES = 160
ORDERS = 6
KMAX = 79
ROWS, COLS = 16, 8
KY, KZ = MODES // ROWS, MODES // COLS
XL, YL = N // ROWS, N // COLS
CHUNKS = 4
XC = XL // CHUNKS
XP = XC // 2
OFFSETS = (0, 20, 40, 64, 84, 104)
TABLES = 8
MESH = pl.DeviceIdType.MESH
bf16, f32 = jnp.bfloat16, jnp.float32


def basis():
    p = np.arange(N)[:, None]
    m = np.arange(MODES)[None, :]
    k = m // 2
    angle = 2.0 * np.pi / N * (p * k % N)
    table = np.where(m % 2 == 0, np.cos(angle), np.sin(angle)) * np.sqrt(np.where(m < 2, 1.0, 2.0) / N)
    table[:, 1] = 0.0
    return table


def halves(table):
    high = np.asarray(table, jnp.bfloat16)
    low = np.asarray(table - high.astype(np.float64), jnp.bfloat16)
    return high, low


def tables():
    s = basis()
    sx = np.zeros((N, 256))
    sx[:, :MODES] = s
    order = np.arange(MODES).reshape(ROWS, KY).T.reshape(-1)
    sy_h, sy_l = halves(s[:, order])
    sy = np.concatenate([sy_h, sy_h, sy_l, np.zeros((N, 32), jnp.bfloat16)], axis=1)
    sz = np.zeros((256, N))
    sz[:120] = s[:, :120].T
    sz[128:168] = s[:, 120:].T
    ya = np.concatenate([sy_h.T, sy_h.T, sy_l.T], axis=1)
    points = np.arange(N).reshape(ROWS, 2, 4, 2).transpose(1, 3, 0, 2)
    xa = np.zeros((2, 2, ROWS, 2, 4, 2, 256))
    for k in range(2):
        xa[:, :, :, k, :, k, :MODES] = s[points]
    xa = xa.reshape(512, 512)
    return (*halves(sx), sy, *halves(sz), *halves(sz.T), ya, *halves(xa))


def split(x):
    high = x.astype(bf16)
    return high, (x - high.astype(f32)).astype(bf16)


def dot(a, b):
    return jnp.dot(a, b, preferred_element_type=f32)


def dot_nt(a, b):
    return lax.dot_general(a, b, (((1,), (1,)), ((), ())), preferred_element_type=f32)


def dot3(x, table_h, table_l):
    high, low = split(x)
    return dot(high, table_h[...]) + (dot(low, table_h[...]) + dot(high, table_l[...]))


def roll(x, shift, axis):
    shift %= x.shape[axis]
    return x if shift == 0 else pltpu.roll(x, shift, axis)


def pair_swap(x, axis):
    even = lax.broadcasted_iota(jnp.int32, x.shape, axis) % 2 == 0
    return jnp.where(even, roll(x, -1, axis), -roll(x, 1, axis))


def kernel(
    a_ref, vel_hbm, vort_hbm, sxh, sxl, *rest,
):
    tables_hbm, (out_ref, *tables_vmem), rest = rest[:TABLES], rest[TABLES : 2 * TABLES + 1], rest[2 * TABLES + 1 :]
    sy, szh, szl, zah, zal, ya, xah, xal = tables_vmem
    (
    a_s, f_s, vel, vort, part, send1, recv1, send2, recv2, send3, recv3, send4, recv4, fin,
    hbm_sem, table_sem, s1s, s1r, s2s, s2r, s3s, s3r, s4s, s4r, own,
    ) = rest
    r, c = lax.axis_index("row"), lax.axis_index("col")

    def row_peer(i):
        return lax.rem(r + i, ROWS)

    def col_peer(i):
        return lax.rem(c + i, COLS)

    barrier = pltpu.get_barrier_semaphore()
    for i in range(1, ROWS):
        pl.semaphore_signal(barrier, 1, device_id=(row_peer(i), c), device_id_type=MESH)
    for i in range(1, COLS):
        pl.semaphore_signal(barrier, 1, device_id=(r, col_peer(i)), device_id_type=MESH)

    def stored(o):
        return (
            pltpu.make_async_copy(vel_hbm.at[o], vel.at[o], hbm_sem.at[0, o]),
            pltpu.make_async_copy(vort_hbm.at[o], vort.at[o], hbm_sem.at[1, o]),
        )

    def table(i):
        return pltpu.make_async_copy(tables_hbm[i], tables_vmem[i], table_sem.at[i])

    for i in range(TABLES):
        table(i).start()
    for o in (1, 5, 2, 4, 3, 0):
        for copy in stored(o):
            copy.start()

    def ds(start, size, unit):
        return pl.ds(pl.multiple_of(start, unit), size)

    def copy1(h, i):
        there = row_peer(i)
        return pltpu.make_async_remote_copy(
            send1.at[:, ds(there * XL + 8 * h, 8, 8), :],
            recv1.at[:, ds(r * XL + 8 * h, 8, 8), :],
            s1s.at[h, i], s1r.at[h, i], device_id=(there, c), device_id_type=MESH,
        )

    def copy2(g, i):
        there = col_peer(i)
        return pltpu.make_async_remote_copy(
            send2.at[pl.ds(g * XC, XC), ds(there * YL, YL, 8), :],
            recv2.at[c, pl.ds(g * XC, XC)],
            s2s.at[g, i], s2r.at[g, i], device_id=(r, there), device_id_type=MESH,
        )

    def copy3(g, i):
        there = col_peer(i)
        return pltpu.make_async_remote_copy(
            send3.at[there, pl.ds(g * XP, XP)],
            recv3.at[pl.ds(g * XP, XP), ds(c * YL, YL, 8), :],
            s3s.at[g, i], s3r.at[g, i], device_id=(r, there), device_id_type=MESH,
        )

    def copy4(h, i):
        there = row_peer(i)
        return pltpu.make_async_remote_copy(
            send4.at[h, :, ds(there * 8, 8, 8), :],
            recv4.at[h, :, ds(r * 8, 8, 8), :],
            s4s.at[h, i], s4r.at[h, i], device_id=(there, c), device_id_type=MESH,
        )

    own1 = pltpu.make_async_copy(send1.at[:, ds(r * XL, XL, 8), :], recv1.at[:, ds(r * XL, XL, 8), :], own.at[0])

    def own4(h):
        return pltpu.make_async_copy(
            send4.at[h, :, ds(r * 8, 8, 8), :], recv4.at[h, :, ds(r * 8, 8, 8), :], own.at[1 + h]
        )

    def own2(g):
        return pltpu.make_async_copy(
            send2.at[pl.ds(g * XC, XC), ds(c * YL, YL, 8), :], recv2.at[c, pl.ds(g * XC, XC)], own.at[3 + g]
        )

    def own3(g):
        return pltpu.make_async_copy(
            send3.at[c, pl.ds(g * XP, XP)], recv3.at[pl.ds(g * XP, XP), ds(c * YL, YL, 8), :], own.at[3 + CHUNKS + g]
        )

    lane = lax.broadcasted_iota(jnp.int32, (24, 256), 1)
    sub = lax.broadcasted_iota(jnp.int32, (24, 256), 0)
    wave_x = (lane // 2).astype(f32) / KMAX
    wave_z = (sub // 2 + c * (KZ // 2)).astype(f32) / KMAX

    def wave_y(pair):
        return (jnp.zeros((24, 256), jnp.int32) + (r * (KY // 2) + pair)).astype(f32) / KMAX

    def diff_x(v):
        return wave_x * pair_swap(v, 1)

    def diff_z(v):
        return wave_z * pair_swap(v, 0)

    a_s[...] = jnp.zeros_like(a_s)
    f_s[...] = jnp.zeros_like(f_s)

    def fields(pair, carry):
        wy = wave_y(pair)
        for k in range(2):
            for i in range(3):
                a_s[k, i, 0:KZ, 0:MODES] = a_ref[i, 2 * pair + k]
        for k in range(2):
            v = [a_s[k, i] for i in range(3)]
            wy_k = wy if k == 0 else -wy
            dy = [wy_k * a_s[1 - k, i] for i in range(3)]
            v += [dy[2] - diff_z(v[1]), diff_z(v[0]) - diff_x(v[2]), diff_x(v[1]) - dy[0]]
            for i in range(6):
                f_s[128 * k + KZ * i : 128 * k + KZ * (i + 1), :] = v[i][0:KZ]
        high, low = split(f_s[...])
        o = dot_nt(sxh[...], high) + (dot_nt(sxh[...], low) + dot_nt(sxl[...], high))
        send1[2 * pair] = o[:, :128]
        send1[2 * pair + 1] = o[:, 128:]
        return carry

    lax.fori_loop(0, KY // 2, fields, 0)

    own1.start()
    pl.semaphore_wait(barrier, ROWS + COLS - 2)
    for h in range(2):
        for i in range(1, ROWS):
            copy1(h, i).start()

    for i in range(TABLES):
        table(i).wait()
    for o in (1, 5, 2, 4, 3):
        for copy in stored(o):
            copy.wait()

    def old_terms(x, carry):
        acc = None
        for o in range(1, ORDERS):
            u = [vel[o, i, x] for i in range(3)]
            w = [vort[ORDERS - o, i, x] for i in range(3)]
            term = [u[1] * w[2] - u[2] * w[1], u[2] * w[0] - u[0] * w[2], u[0] * w[1] - u[1] * w[0]]
            acc = term if acc is None else [p + q for p, q in zip(acc, term)]
        for i in range(3):
            part[i, x] = acc[i]
        return carry

    lax.fori_loop(0, XL, old_terms, 0)
    for copy in stored(0):
        copy.wait()

    def synth_y(xp, carry):
        t = []
        for k in range(2):
            rows = pl.ds(2 * xp + k, ROWS, stride=XL)
            t.append(jnp.concatenate([recv1[m, rows, :] for m in range(KY)], axis=0))
        high, low = split(jnp.concatenate(t, axis=1))
        rhs = jnp.concatenate([high, low, high, jnp.zeros((32, 256), bf16)], axis=0)
        o = dot(sy[...], rhs)
        send2[2 * xp] = o[:, :128]
        send2[2 * xp + 1] = o[:, 128:]
        return carry

    own1.wait()
    for h in range(2):
        for i in range(1, ROWS):
            copy1(h, i).wait_recv()
        for g in range(h * CHUNKS // 2, (h + 1) * CHUNKS // 2):
            lax.fori_loop(g * XP, (g + 1) * XP, synth_y, 0)
            own2(g).start()
            for i in range(1, COLS):
                copy2(g, i).start()

    lane_y = lax.broadcasted_iota(jnp.int32, (YL, 128), 1)

    def place(first):
        q = lane_y - first
        return jnp.where(q < 0, q + 128, q)

    def middle(xp, carry):
        sums = []
        for k in range(2):
            x = 2 * xp + k
            blocks = [roll(recv2[m, x], KZ * (m % 6), 1) for m in range(COLS)]
            tile1, tile2 = [], []
            for i in range(6):
                q = place(KZ * i)
                t = blocks[0]
                for m in range(1, 6):
                    t = jnp.where(q >= KZ * m, blocks[m], t)
                tile1.append(roll(t, -KZ * i, 1))
                tile2.append(roll(jnp.where(q >= KZ, blocks[7], blocks[6]), -KZ * i, 1))
            modes = jnp.concatenate([jnp.concatenate(tile1, axis=0), jnp.concatenate(tile2, axis=0)], axis=1)
            new = dot3(modes, szh, szl)
            u = [new[YL * i : YL * (i + 1)] for i in range(3)]
            w = [new[YL * i : YL * (i + 1)] for i in range(3, 6)]
            v0 = [vel[0, i, x] for i in range(3)]
            w0 = [vort[0, i, x] for i in range(3)]
            for i in range(3):
                a, b = (i + 1) % 3, (i + 2) % 3
                sums.append(part[i, x] + ((u[a] * w0[b] - u[b] * w0[a]) + (v0[a] * w[b] - v0[b] * w[a])))
        o = dot3(jnp.concatenate(sums, axis=0), zah, zal)
        out = [o[YL * j : YL * (j + 1)] for j in range(6)]
        for half in range(2):
            rolled = [roll(out[j][:, 128 * half : 128 * half + 128], OFFSETS[j], 1) for j in range(6)]
            for m in range(6 if half == 0 else 2):
                q = place(KZ * m)
                t = rolled[0]
                for j in range(1, 6):
                    t = jnp.where(q >= OFFSETS[j], rolled[j], t)
                send3[6 * half + m, xp] = roll(t, -KZ * m, 1)
        return carry

    for g in range(CHUNKS):
        own2(g).wait()
        for i in range(1, COLS):
            copy2(g, i).wait_recv()
        lax.fori_loop(g * XP, (g + 1) * XP, middle, 0)
        own3(g).start()
        for i in range(1, COLS):
            copy3(g, i).start()

    def analyze_y(h, xq):
        high, low = split(jnp.concatenate([recv3[2 * xq], recv3[2 * xq + 1]], axis=1))
        o = dot(ya[...], jnp.concatenate([high, low, high], axis=0))
        for k in range(2):
            for m in range(KY):
                rows = pl.ds(4 * (m % 2) + 2 * xq - 4 * h + k, ROWS, stride=8)
                send4[h, m // 2, rows, :] = o[ROWS * m : ROWS * (m + 1), 128 * k : 128 * k + 128]

    def analyze_x(h):
        rows = []
        for m in range(KY // 2):
            t = recv4[h, m].T
            rows.append(jnp.concatenate([t[0:64], t[64:128]], axis=1))
        high, low = split(jnp.concatenate(rows, axis=0))
        part_h, part_l = xah[256 * h : 256 * h + 256, :], xal[256 * h : 256 * h + 256, :]
        return dot(high, part_h) + (dot(low, part_h) + dot(high, part_l))

    for h in range(2):
        for g in range(h * CHUNKS // 2, (h + 1) * CHUNKS // 2):
            own3(g).wait()
            for i in range(1, COLS):
                copy3(g, i).wait_recv()
            for q in range(g * XP // 2, (g + 1) * XP // 2):
                analyze_y(h, q)
        own4(h).start()
        for i in range(1, ROWS):
            copy4(h, i).start()
    for h in range(2):
        own4(h).wait()
        for i in range(1, ROWS):
            copy4(h, i).wait_recv()
        if h == 0:
            fin[...] = analyze_x(0)
        else:
            fin[...] += analyze_x(1)

    def finish(pair, carry):
        first = 64 * pair
        s = [
            [fin[first + KZ * i : first + KZ * i + 24, 256 * k : 256 * k + 256] for i in range(3)] for k in range(2)
        ]
        wy = wave_y(pair)
        square = wy**2 + wave_z**2 + wave_x**2
        some = square > 0
        safe = jnp.where(some, square, 1.0)
        potential = []
        for k in range(2):
            wy_k = wy if k == 0 else -wy
            divergence = diff_x(s[k][0]) + wy_k * s[1 - k][1] + diff_z(s[k][2])
            potential.append(jnp.where(some, divergence / safe, 0.0))
        for k in range(2):
            wy_k = wy if k == 0 else -wy
            slopes = (diff_x(potential[k]), wy_k * potential[1 - k], diff_z(potential[k]))
            for i in range(3):
                out_ref[i, 2 * pair + k] = (s[k][i] + slopes[i])[0:KZ, 0:MODES]
        return carry

    for pair in range(KY // 2):
        finish(pair, 0)

    for h in range(2):
        for i in range(1, ROWS):
            copy1(h, i).wait_send()
            copy4(h, i).wait_send()
    for g in range(CHUNKS):
        for i in range(1, COLS):
            copy2(g, i).wait_send()
            copy3(g, i).wait_send()


def shards(new_velocity, stored_velocity, stored_vorticity):
    consts = tables()
    vmem = pl.BlockSpec(memory_space=pltpu.VMEM)
    hbm = pl.BlockSpec(memory_space=pl.ANY)
    dma = pltpu.SemaphoreType.DMA
    sums = pl.pallas_call(
        kernel,
        out_shape=jax.ShapeDtypeStruct((3, KY, KZ, MODES), f32),
        in_specs=[vmem, hbm, hbm, vmem, vmem] + [hbm] * TABLES,
        out_specs=vmem,
        scratch_shapes=[
            *(pltpu.VMEM(t.shape, bf16) for t in consts[2:]),
            pltpu.VMEM((2, 3, 24, 256), f32),
            pltpu.VMEM((256, 256), f32),
            pltpu.VMEM((ORDERS, 3, XL, YL, N), f32),
            pltpu.VMEM((ORDERS, 3, XL, YL, N), f32),
            pltpu.VMEM((3, XL, YL, N), f32),
            pltpu.VMEM((KY, N, 128), f32),
            pltpu.VMEM((KY, N, 128), f32),
            pltpu.VMEM((XL, N, 128), f32),
            pltpu.VMEM((COLS, XL, YL, 128), f32),
            pltpu.VMEM((COLS, XL // 2, YL, 128), f32),
            pltpu.VMEM((XL // 2, N, 128), f32),
            pltpu.VMEM((2, KY // 2, 128, 128), f32),
            pltpu.VMEM((2, KY // 2, 128, 128), f32),
            pltpu.VMEM((KY // 2 * 64, 512), f32),
            dma((2, ORDERS)),
            dma((TABLES,)),
            dma((2, ROWS)),
            dma((2, ROWS)),
            dma((CHUNKS, COLS)),
            dma((CHUNKS, COLS)),
            dma((CHUNKS, COLS)),
            dma((CHUNKS, COLS)),
            dma((2, ROWS)),
            dma((2, ROWS)),
            dma((3 + 2 * CHUNKS,)),
        ],
        compiler_params=pltpu.CompilerParams(
            collective_id=0, has_side_effects=True, vmem_limit_bytes=60 * 2**20
        ),
        name="euler_order",
    )(new_velocity, stored_velocity, stored_vorticity, *map(jnp.asarray, consts))
    return sums / (ORDERS + 1)


def solution(mesh):
    return jax.shard_map(
        shards,
        mesh=mesh,
        in_specs=(
            P(None, "row", "col", None),
            P(None, None, "row", "col", None),
            P(None, None, "row", "col", None),
        ),
        out_specs=P(None, "row", "col", None),
        check_vma=False,
    )
```

```python
import jax
import jax.numpy as jnp
import numpy as np
from jax import lax
from jax.experimental import pallas as pl
from jax.experimental.pallas import tpu as pltpu
from jax.sharding import PartitionSpec as P

N = 256
MODES = 160
ORDERS = 6
KMAX = 79
ROWS, COLS = 16, 8
KY, KZ = MODES // ROWS, MODES // COLS
XL, YL = N // ROWS, N // COLS
CHUNKS = 4
XC = XL // CHUNKS
XP = XC // 2
OFFSETS = (0, 20, 40, 64, 84, 104)
TILES = 8
TABLES = 8
MESH = pl.DeviceIdType.MESH
bf16, f32 = jnp.bfloat16, jnp.float32


def basis():
    p = np.arange(N)[:, None]
    m = np.arange(MODES)[None, :]
    k = m // 2
    angle = 2.0 * np.pi / N * (p * k % N)
    table = np.where(m % 2 == 0, np.cos(angle), np.sin(angle)) * np.sqrt(np.where(m < 2, 1.0, 2.0) / N)
    table[:, 1] = 0.0
    return table


def halves(table):
    high = np.asarray(table, jnp.bfloat16)
    low = np.asarray(table - high.astype(np.float64), jnp.bfloat16)
    return high, low


def tables():
    s = basis()
    sx = np.zeros((N, 256))
    sx[:, :MODES] = s
    order = np.arange(MODES).reshape(ROWS, KY).T.reshape(-1)
    sy_h, sy_l = halves(s[:, order])
    sy = np.concatenate([sy_h, sy_h, sy_l, np.zeros((N, 32), jnp.bfloat16)], axis=1)
    sz = np.zeros((256, N))
    sz[:120] = s[:, :120].T
    sz[128:168] = s[:, 120:].T
    ya = np.concatenate([sy_h.T, sy_h.T, sy_l.T], axis=1)
    points = np.arange(N).reshape(ROWS, 2, 4, 2).transpose(1, 3, 0, 2)
    xa = np.zeros((2, 2, ROWS, 2, 4, 2, 256))
    for k in range(2):
        xa[:, :, :, k, :, k, :MODES] = s[points]
    xa = xa.reshape(512, 512)
    return (*halves(sx), sy, *halves(sz), *halves(sz.T), ya, *halves(xa))


def split(x):
    high = x.astype(bf16)
    return high, (x - high.astype(f32)).astype(bf16)


def dot(a, b):
    return jnp.dot(a, b, preferred_element_type=f32)


def dot_nt(a, b):
    return lax.dot_general(a, b, (((1,), (1,)), ((), ())), preferred_element_type=f32)


def dot3(x, table_h, table_l):
    high, low = split(x)
    return dot(high, table_h[...]) + (dot(low, table_h[...]) + dot(high, table_l[...]))


def roll(x, shift, axis):
    shift %= x.shape[axis]
    return x if shift == 0 else pltpu.roll(x, shift, axis)


def pair_swap(x, axis):
    even = lax.broadcasted_iota(jnp.int32, x.shape, axis) % 2 == 0
    return jnp.where(even, roll(x, -1, axis), -roll(x, 1, axis))


def kernel(
    a_ref, vel_hbm, vort_hbm, sxh, sxl, *rest,
):
    tables_hbm, (out_ref, *tables_vmem), rest = rest[:TABLES], rest[TABLES : 2 * TABLES + 1], rest[2 * TABLES + 1 :]
    sy, szh, szl, zah, zal, ya, xah, xal = tables_vmem
    (
    a_s, f_s, vel, vort, part, send1, recv1, send2, recv2, send3, recv3, send4, recv4, fin,
    hbm_sem, table_sem, s1s, s1r, s2s, s2r, s3s, s3r, s4s, s4r, own,
    ) = rest
    r, c = lax.axis_index("row"), lax.axis_index("col")

    def row_peer(i):
        return lax.rem(r + i, ROWS)

    def col_peer(i):
        return lax.rem(c + i, COLS)

    barrier = pltpu.get_barrier_semaphore()
    for i in range(1, ROWS):
        pl.semaphore_signal(barrier, 1, device_id=(row_peer(i), c), device_id_type=MESH)
    for i in range(1, COLS):
        pl.semaphore_signal(barrier, 1, device_id=(r, col_peer(i)), device_id_type=MESH)

    def stored(o):
        return (
            pltpu.make_async_copy(vel_hbm.at[o], vel.at[o], hbm_sem.at[0, o]),
            pltpu.make_async_copy(vort_hbm.at[o], vort.at[o], hbm_sem.at[1, o]),
        )

    def table(i):
        return pltpu.make_async_copy(tables_hbm[i], tables_vmem[i], table_sem.at[i])

    for i in range(TABLES):
        table(i).start()
    for o in (1, 5, 2, 4, 3, 0):
        for copy in stored(o):
            copy.start()

    def ds(start, size, unit):
        return pl.ds(pl.multiple_of(start, unit), size)

    def copy1(h, i):
        there = row_peer(i)
        return pltpu.make_async_remote_copy(
            send1.at[:, ds(there * XL + 8 * h, 8, 8), :],
            recv1.at[:, ds(r * XL + 8 * h, 8, 8), :],
            s1s.at[h, i], s1r.at[h, i], device_id=(there, c), device_id_type=MESH,
        )

    def copy2(g, i):
        there = col_peer(i)
        return pltpu.make_async_remote_copy(
            send2.at[pl.ds(g * XC, XC), ds(there * YL, YL, 8), :],
            recv2.at[c, pl.ds(g * XC, XC)],
            s2s.at[g, i], s2r.at[g, i], device_id=(r, there), device_id_type=MESH,
        )

    def copy3(g, i):
        there = col_peer(i)
        return pltpu.make_async_remote_copy(
            send3.at[there, pl.ds(g * XP, XP)],
            recv3.at[pl.ds(g * XP, XP), ds(c * YL, YL, 8), :],
            s3s.at[g, i], s3r.at[g, i], device_id=(r, there), device_id_type=MESH,
        )

    def copy4(h, i):
        there = row_peer(i)
        return pltpu.make_async_remote_copy(
            send4.at[h, :, ds(there * 8, 8, 8), :],
            recv4.at[h, :, ds(r * 8, 8, 8), :],
            s4s.at[h, i], s4r.at[h, i], device_id=(there, c), device_id_type=MESH,
        )

    own1 = pltpu.make_async_copy(send1.at[:, ds(r * XL, XL, 8), :], recv1.at[:, ds(r * XL, XL, 8), :], own.at[0])

    def own4(h):
        return pltpu.make_async_copy(
            send4.at[h, :, ds(r * 8, 8, 8), :], recv4.at[h, :, ds(r * 8, 8, 8), :], own.at[1 + h]
        )

    def own2(g):
        return pltpu.make_async_copy(
            send2.at[pl.ds(g * XC, XC), ds(c * YL, YL, 8), :], recv2.at[c, pl.ds(g * XC, XC)], own.at[3 + g]
        )

    def own3(g):
        return pltpu.make_async_copy(
            send3.at[c, pl.ds(g * XP, XP)], recv3.at[pl.ds(g * XP, XP), ds(c * YL, YL, 8), :], own.at[3 + CHUNKS + g]
        )

    lane = lax.broadcasted_iota(jnp.int32, (24, 256), 1)
    sub = lax.broadcasted_iota(jnp.int32, (24, 256), 0)
    wave_x = (lane // 2).astype(f32) / KMAX
    wave_z = (sub // 2 + c * (KZ // 2)).astype(f32) / KMAX

    def wave_y(pair):
        return (jnp.zeros((24, 256), jnp.int32) + (r * (KY // 2) + pair)).astype(f32) / KMAX

    def diff_x(v):
        return wave_x * pair_swap(v, 1)

    def diff_z(v):
        return wave_z * pair_swap(v, 0)

    a_s[...] = jnp.zeros_like(a_s)
    f_s[...] = jnp.zeros_like(f_s)
    for m in range(KY):
        for i in range(3):
            a_s[i, 0:KZ, 0:MODES] = a_ref[i, m]
        v = [a_s[i] for i in range(3)]
        v += [diff_x(v[2]), diff_x(v[1])]
        for i in range(5):
            first = KZ * (5 * m + i)
            f_s[first : first + KZ, :] = v[i][0:KZ]

    for t in range(TILES // 2):
        high, low = split(f_s[256 * t : 256 * t + 256, :])
        o = dot_nt(sxh[...], high) + (dot_nt(sxh[...], low) + dot_nt(sxl[...], high))
        send1[2 * t] = o[:, :128]
        send1[2 * t + 1] = o[:, 128:]

    own1.start()
    pl.semaphore_wait(barrier, ROWS + COLS - 2)
    for h in range(2):
        for i in range(1, ROWS):
            copy1(h, i).start()

    for i in range(TABLES):
        table(i).wait()
    for o in (1, 5, 2, 4, 3):
        for copy in stored(o):
            copy.wait()

    def old_terms(x, carry):
        acc = None
        for o in range(1, ORDERS):
            u = [vel[o, i, x] for i in range(3)]
            w = [vort[ORDERS - o, i, x] for i in range(3)]
            term = [u[1] * w[2] - u[2] * w[1], u[2] * w[0] - u[0] * w[2], u[0] * w[1] - u[1] * w[0]]
            acc = term if acc is None else [p + q for p, q in zip(acc, term)]
        for i in range(3):
            part[i, x] = acc[i]
        return carry

    lax.fori_loop(0, XL, old_terms, 0)
    for copy in stored(0):
        copy.wait()

    lane_r = lax.broadcasted_iota(jnp.int32, (ROWS, 128), 1)
    sub_r = lax.broadcasted_iota(jnp.int32, (ROWS, 128), 0)
    slope_z = (lane_r % KZ // 2 + c * (KZ // 2)).astype(f32) / KMAX

    def synth_y(xp, carry):
        t = []
        for k in range(2):
            rows = pl.ds(2 * xp + k, ROWS, stride=XL)
            tiles = [recv1[m, rows, :] for m in range(TILES)]
            sent = []
            for m in range(KY):
                tile, first = divmod(5 * KZ * m, 128)
                block = roll(tiles[tile], -first, 1)
                if first + 5 * KZ > 128:
                    block = jnp.where(lane_r < 128 - first, block, roll(tiles[tile + 1], -first, 1))
                sent.append(block)
            modes = []
            for m in range(KY):
                slope_y = (sub_r * (KY // 2) + m // 2).astype(f32) / KMAX
                dy = slope_y * (-sent[m - 1] if m % 2 else sent[m + 1])
                dz = slope_z * pair_swap(sent[m], 1)
                x_terms = roll(sent[m], KZ, 1)
                curl_x = roll(dy, KZ, 1) - roll(dz, 2 * KZ, 1)
                curl_y = roll(dz, 4 * KZ, 1) - x_terms
                curl_z = x_terms - roll(dy, 5 * KZ, 1)
                modes.append(
                    jnp.where(
                        lane_r < 3 * KZ,
                        sent[m],
                        jnp.where(lane_r < 4 * KZ, curl_x, jnp.where(lane_r < 5 * KZ, curl_y, curl_z)),
                    )
                )
            t.append(jnp.concatenate(modes, axis=0))
        high, low = split(jnp.concatenate(t, axis=1))
        rhs = jnp.concatenate([high, low, high, jnp.zeros((32, 256), bf16)], axis=0)
        o = dot(sy[...], rhs)
        send2[2 * xp] = o[:, :128]
        send2[2 * xp + 1] = o[:, 128:]
        return carry

    own1.wait()
    for h in range(2):
        for i in range(1, ROWS):
            copy1(h, i).wait_recv()
        for g in range(h * CHUNKS // 2, (h + 1) * CHUNKS // 2):
            lax.fori_loop(g * XP, (g + 1) * XP, synth_y, 0)
            own2(g).start()
            for i in range(1, COLS):
                copy2(g, i).start()

    lane_y = lax.broadcasted_iota(jnp.int32, (YL, 128), 1)

    def place(first):
        q = lane_y - first
        return jnp.where(q < 0, q + 128, q)

    def middle(xp, carry):
        sums = []
        for k in range(2):
            x = 2 * xp + k
            blocks = [roll(recv2[m, x], KZ * (m % 6), 1) for m in range(COLS)]
            tile1, tile2 = [], []
            for i in range(6):
                q = place(KZ * i)
                t = blocks[0]
                for m in range(1, 6):
                    t = jnp.where(q >= KZ * m, blocks[m], t)
                tile1.append(roll(t, -KZ * i, 1))
                tile2.append(roll(jnp.where(q >= KZ, blocks[7], blocks[6]), -KZ * i, 1))
            modes = jnp.concatenate([jnp.concatenate(tile1, axis=0), jnp.concatenate(tile2, axis=0)], axis=1)
            new = dot3(modes, szh, szl)
            u = [new[YL * i : YL * (i + 1)] for i in range(3)]
            w = [new[YL * i : YL * (i + 1)] for i in range(3, 6)]
            v0 = [vel[0, i, x] for i in range(3)]
            w0 = [vort[0, i, x] for i in range(3)]
            for i in range(3):
                a, b = (i + 1) % 3, (i + 2) % 3
                sums.append(part[i, x] + ((u[a] * w0[b] - u[b] * w0[a]) + (v0[a] * w[b] - v0[b] * w[a])))
        o = dot3(jnp.concatenate(sums, axis=0), zah, zal)
        out = [o[YL * j : YL * (j + 1)] for j in range(6)]
        for half in range(2):
            rolled = [roll(out[j][:, 128 * half : 128 * half + 128], OFFSETS[j], 1) for j in range(6)]
            for m in range(6 if half == 0 else 2):
                q = place(KZ * m)
                t = rolled[0]
                for j in range(1, 6):
                    t = jnp.where(q >= OFFSETS[j], rolled[j], t)
                send3[6 * half + m, xp] = roll(t, -KZ * m, 1)
        return carry

    for g in range(CHUNKS):
        own2(g).wait()
        for i in range(1, COLS):
            copy2(g, i).wait_recv()
        lax.fori_loop(g * XP, (g + 1) * XP, middle, 0)
        own3(g).start()
        for i in range(1, COLS):
            copy3(g, i).start()

    def analyze_y(h, xq):
        high, low = split(jnp.concatenate([recv3[2 * xq], recv3[2 * xq + 1]], axis=1))
        o = dot(ya[...], jnp.concatenate([high, low, high], axis=0))
        for k in range(2):
            for m in range(KY):
                rows = pl.ds(4 * (m % 2) + 2 * xq - 4 * h + k, ROWS, stride=8)
                send4[h, m // 2, rows, :] = o[ROWS * m : ROWS * (m + 1), 128 * k : 128 * k + 128]

    def analyze_x(h):
        rows = []
        for m in range(KY // 2):
            t = recv4[h, m].T
            rows.append(jnp.concatenate([t[0:64], t[64:128]], axis=1))
        high, low = split(jnp.concatenate(rows, axis=0))
        part_h, part_l = xah[256 * h : 256 * h + 256, :], xal[256 * h : 256 * h + 256, :]
        return dot(high, part_h) + (dot(low, part_h) + dot(high, part_l))

    for h in range(2):
        for g in range(h * CHUNKS // 2, (h + 1) * CHUNKS // 2):
            own3(g).wait()
            for i in range(1, COLS):
                copy3(g, i).wait_recv()
            for q in range(g * XP // 2, (g + 1) * XP // 2):
                analyze_y(h, q)
        own4(h).start()
        for i in range(1, ROWS):
            copy4(h, i).start()
    for h in range(2):
        own4(h).wait()
        for i in range(1, ROWS):
            copy4(h, i).wait_recv()
        if h == 0:
            fin[...] = analyze_x(0)
        else:
            fin[...] += analyze_x(1)

    def finish(pair, carry):
        first = 64 * pair
        s = [
            [fin[first + KZ * i : first + KZ * i + 24, 256 * k : 256 * k + 256] for i in range(3)] for k in range(2)
        ]
        wy = wave_y(pair)
        square = wy**2 + wave_z**2 + wave_x**2
        some = square > 0
        safe = jnp.where(some, square, 1.0)
        potential = []
        for k in range(2):
            wy_k = wy if k == 0 else -wy
            divergence = diff_x(s[k][0]) + wy_k * s[1 - k][1] + diff_z(s[k][2])
            potential.append(jnp.where(some, divergence / safe, 0.0))
        for k in range(2):
            wy_k = wy if k == 0 else -wy
            slopes = (diff_x(potential[k]), wy_k * potential[1 - k], diff_z(potential[k]))
            for i in range(3):
                out_ref[i, 2 * pair + k] = (s[k][i] + slopes[i])[0:KZ, 0:MODES]
        return carry

    for pair in range(KY // 2):
        finish(pair, 0)

    for h in range(2):
        for i in range(1, ROWS):
            copy1(h, i).wait_send()
            copy4(h, i).wait_send()
    for g in range(CHUNKS):
        for i in range(1, COLS):
            copy2(g, i).wait_send()
            copy3(g, i).wait_send()


def shards(new_velocity, stored_velocity, stored_vorticity):
    consts = tables()
    vmem = pl.BlockSpec(memory_space=pltpu.VMEM)
    hbm = pl.BlockSpec(memory_space=pl.ANY)
    dma = pltpu.SemaphoreType.DMA
    sums = pl.pallas_call(
        kernel,
        out_shape=jax.ShapeDtypeStruct((3, KY, KZ, MODES), f32),
        in_specs=[vmem, hbm, hbm, vmem, vmem] + [hbm] * TABLES,
        out_specs=vmem,
        scratch_shapes=[
            *(pltpu.VMEM(t.shape, bf16) for t in consts[2:]),
            pltpu.VMEM((3, 24, 256), f32),
            pltpu.VMEM((128 * TILES, 256), f32),
            pltpu.VMEM((ORDERS, 3, XL, YL, N), f32),
            pltpu.VMEM((ORDERS, 3, XL, YL, N), f32),
            pltpu.VMEM((3, XL, YL, N), f32),
            pltpu.VMEM((TILES, N, 128), f32),
            pltpu.VMEM((TILES, N, 128), f32),
            pltpu.VMEM((XL, N, 128), f32),
            pltpu.VMEM((COLS, XL, YL, 128), f32),
            pltpu.VMEM((COLS, XL // 2, YL, 128), f32),
            pltpu.VMEM((XL // 2, N, 128), f32),
            pltpu.VMEM((2, KY // 2, 128, 128), f32),
            pltpu.VMEM((2, KY // 2, 128, 128), f32),
            pltpu.VMEM((KY // 2 * 64, 512), f32),
            dma((2, ORDERS)),
            dma((TABLES,)),
            dma((2, ROWS)),
            dma((2, ROWS)),
            dma((CHUNKS, COLS)),
            dma((CHUNKS, COLS)),
            dma((CHUNKS, COLS)),
            dma((CHUNKS, COLS)),
            dma((2, ROWS)),
            dma((2, ROWS)),
            dma((3 + 2 * CHUNKS,)),
        ],
        compiler_params=pltpu.CompilerParams(
            collective_id=0, has_side_effects=True, vmem_limit_bytes=60 * 2**20
        ),
        name="euler_order",
    )(new_velocity, stored_velocity, stored_vorticity, *map(jnp.asarray, consts))
    return sums / (ORDERS + 1)


def solution(mesh):
    return jax.shard_map(
        shards,
        mesh=mesh,
        in_specs=(
            P(None, "row", "col", None),
            P(None, None, "row", "col", None),
            P(None, None, "row", "col", None),
        ),
        out_specs=P(None, "row", "col", None),
        check_vma=False,
    )
```

```python
import jax
import jax.numpy as jnp
import numpy as np
from jax import lax
from jax.experimental import pallas as pl
from jax.experimental.pallas import tpu as pltpu
from jax.sharding import PartitionSpec as P

N = 256
MODES = 160
ORDERS = 6
KMAX = 79
ROWS, COLS = 16, 8
KY, KZ = MODES // ROWS, MODES // COLS
XL, YL = N // ROWS, N // COLS
CHUNKS = 4
XC = XL // CHUNKS
XP = XC // 2
OFFSETS = (0, 20, 40, 64, 84, 104)
TILES = 8
TABLES = 10
MESH = pl.DeviceIdType.MESH
bf16, f32 = jnp.bfloat16, jnp.float32


def basis():
    p = np.arange(N)[:, None]
    m = np.arange(MODES)[None, :]
    k = m // 2
    angle = 2.0 * np.pi / N * (p * k % N)
    table = np.where(m % 2 == 0, np.cos(angle), np.sin(angle)) * np.sqrt(np.where(m < 2, 1.0, 2.0) / N)
    table[:, 1] = 0.0
    return table


def halves(table):
    high = np.asarray(table, jnp.bfloat16)
    low = np.asarray(table - high.astype(np.float64), jnp.bfloat16)
    return high, low


def tables():
    s = basis()
    sx = np.zeros((N, 256))
    sx[:, :MODES] = s.reshape(ROWS, 2, 8, MODES).transpose(1, 0, 2, 3).reshape(N, MODES)
    order = np.arange(MODES).reshape(ROWS, KY).T.reshape(-1)
    sy_h, sy_l = halves(s[:, order])
    sy = np.concatenate([sy_h, sy_h, sy_l, np.zeros((N, 32), jnp.bfloat16)], axis=1)
    sz = np.zeros((256, N))
    sz[:120] = s[:, :120].T
    sz[128:168] = s[:, 120:].T
    ya = np.concatenate([sy_h.T, sy_h.T, sy_l.T], axis=1)
    points = np.arange(N).reshape(ROWS, 2, 4, 2).transpose(1, 3, 0, 2)
    xa = np.zeros((2, 2, ROWS, 2, 4, 2, 256))
    for k in range(2):
        xa[:, :, :, k, :, k, :MODES] = s[points]
    xa = xa.reshape(512, 512)
    return (*halves(sx), sy, *halves(sz), *halves(sz.T), ya, *halves(xa))


def split(x):
    high = x.astype(bf16)
    return high, (x - high.astype(f32)).astype(bf16)


def dot(a, b):
    return jnp.dot(a, b, preferred_element_type=f32)


def dot_nt(a, b):
    return lax.dot_general(a, b, (((1,), (1,)), ((), ())), preferred_element_type=f32)


def dot3(x, table_h, table_l):
    high, low = split(x)
    return dot(high, table_h[...]) + (dot(low, table_h[...]) + dot(high, table_l[...]))


def roll(x, shift, axis):
    shift %= x.shape[axis]
    return x if shift == 0 else pltpu.roll(x, shift, axis)


def pair_swap(x, axis):
    even = lax.broadcasted_iota(jnp.int32, x.shape, axis) % 2 == 0
    return jnp.where(even, roll(x, -1, axis), -roll(x, 1, axis))


def kernel(
    a_hbm, vel_hbm, vort_hbm, *rest,
):
    tables_hbm, (out_ref, *tables_vmem), rest = rest[:TABLES], rest[TABLES : 2 * TABLES + 1], rest[2 * TABLES + 1 :]
    sxh, sxl, sy, szh, szl, zah, zal, ya, xah, xal = tables_vmem
    (
    a_ref, a_s, f_s, vel, vort, part, send1, recv1, send2, recv2, send3, recv3, send4, recv4, fin,
    hbm_sem, a_sem, table_sem, s1s, s1r, s2s, s2r, s3s, s3r, s4s, s4r, own,
    ) = rest
    r, c = lax.axis_index("row"), lax.axis_index("col")

    def row_peer(i):
        return lax.rem(r + i, ROWS)

    def col_peer(i):
        return lax.rem(c + i, COLS)

    barrier = pltpu.get_barrier_semaphore()
    for i in range(1, ROWS):
        pl.semaphore_signal(barrier, 1, device_id=(row_peer(i), c), device_id_type=MESH)
    for i in range(1, COLS):
        pl.semaphore_signal(barrier, 1, device_id=(r, col_peer(i)), device_id_type=MESH)

    def stored(o):
        return (
            pltpu.make_async_copy(vel_hbm.at[o], vel.at[o], hbm_sem.at[0, o]),
            pltpu.make_async_copy(vort_hbm.at[o], vort.at[o], hbm_sem.at[1, o]),
        )

    def table(i):
        return pltpu.make_async_copy(tables_hbm[i], tables_vmem[i], table_sem.at[i])

    first = pltpu.make_async_copy(a_hbm, a_ref, a_sem)
    first.start()
    table(0).start()
    table(1).start()

    def ds(start, size, unit):
        return pl.ds(pl.multiple_of(start, unit), size)

    def copy1(h, i):
        there = row_peer(i)
        return pltpu.make_async_remote_copy(
            send1.at[:, h, ds(there * 8, 8, 8), :],
            recv1.at[:, h, ds(r * 8, 8, 8), :],
            s1s.at[h, i], s1r.at[h, i], device_id=(there, c), device_id_type=MESH,
        )

    def copy2(g, i):
        there = col_peer(i)
        return pltpu.make_async_remote_copy(
            send2.at[pl.ds(g * XC, XC), ds(there * YL, YL, 8), :],
            recv2.at[c, pl.ds(g * XC, XC)],
            s2s.at[g, i], s2r.at[g, i], device_id=(r, there), device_id_type=MESH,
        )

    def copy3(g, i):
        there = col_peer(i)
        return pltpu.make_async_remote_copy(
            send3.at[there, pl.ds(g * XP, XP)],
            recv3.at[pl.ds(g * XP, XP), ds(c * YL, YL, 8), :],
            s3s.at[g, i], s3r.at[g, i], device_id=(r, there), device_id_type=MESH,
        )

    def copy4(h, i):
        there = row_peer(i)
        return pltpu.make_async_remote_copy(
            send4.at[h, :, ds(there * 8, 8, 8), :],
            recv4.at[h, :, ds(r * 8, 8, 8), :],
            s4s.at[h, i], s4r.at[h, i], device_id=(there, c), device_id_type=MESH,
        )

    def own1(h):
        return pltpu.make_async_copy(
            send1.at[:, h, ds(r * 8, 8, 8), :], recv1.at[:, h, ds(r * 8, 8, 8), :], own.at[h]
        )

    def own4(h):
        return pltpu.make_async_copy(
            send4.at[h, :, ds(r * 8, 8, 8), :], recv4.at[h, :, ds(r * 8, 8, 8), :], own.at[2 + h]
        )

    def own2(g):
        return pltpu.make_async_copy(
            send2.at[pl.ds(g * XC, XC), ds(c * YL, YL, 8), :], recv2.at[c, pl.ds(g * XC, XC)], own.at[4 + g]
        )

    def own3(g):
        return pltpu.make_async_copy(
            send3.at[c, pl.ds(g * XP, XP)], recv3.at[pl.ds(g * XP, XP), ds(c * YL, YL, 8), :], own.at[4 + CHUNKS + g]
        )

    lane = lax.broadcasted_iota(jnp.int32, (24, 256), 1)
    sub = lax.broadcasted_iota(jnp.int32, (24, 256), 0)
    wave_x = (lane // 2).astype(f32) / KMAX
    wave_z = (sub // 2 + c * (KZ // 2)).astype(f32) / KMAX

    def wave_y(pair):
        return (jnp.zeros((24, 256), jnp.int32) + (r * (KY // 2) + pair)).astype(f32) / KMAX

    def diff_x(v):
        return wave_x * pair_swap(v, 1)

    def diff_z(v):
        return wave_z * pair_swap(v, 0)

    a_s[...] = jnp.zeros_like(a_s)
    f_s[...] = jnp.zeros_like(f_s)
    first.wait()
    for m in range(KY):
        for i in range(3):
            a_s[i, 0:KZ, 0:MODES] = a_ref[i, m]
        v = [a_s[i] for i in range(3)]
        v += [diff_x(v[2]), diff_x(v[1])]
        for i in range(5):
            first = KZ * (5 * m + i)
            f_s[first : first + KZ, :] = v[i][0:KZ]

    table(0).wait()
    table(1).wait()
    for i in range(2, TABLES):
        table(i).start()
    for o in (1, 5, 2, 4, 3, 0):
        for copy in stored(o):
            copy.start()
    for h in range(2):
        part_h, part_l = sxh[128 * h : 128 * h + 128, :], sxl[128 * h : 128 * h + 128, :]
        for t in range(TILES // 2):
            high, low = split(f_s[256 * t : 256 * t + 256, :])
            o = dot_nt(part_h, high) + (dot_nt(part_h, low) + dot_nt(part_l, high))
            send1[2 * t, h] = o[:, :128]
            send1[2 * t + 1, h] = o[:, 128:]
        own1(h).start()
        if h == 0:
            pl.semaphore_wait(barrier, ROWS + COLS - 2)
        for i in range(1, ROWS):
            copy1(h, i).start()

    for i in range(2, TABLES):
        table(i).wait()
    for o in (1, 5, 2, 4, 3):
        for copy in stored(o):
            copy.wait()

    def old_terms(x, carry):
        acc = None
        for o in range(1, ORDERS):
            u = [vel[o, i, x] for i in range(3)]
            w = [vort[ORDERS - o, i, x] for i in range(3)]
            term = [u[1] * w[2] - u[2] * w[1], u[2] * w[0] - u[0] * w[2], u[0] * w[1] - u[1] * w[0]]
            acc = term if acc is None else [p + q for p, q in zip(acc, term)]
        for i in range(3):
            part[i, x] = acc[i]
        return carry

    lax.fori_loop(0, XL, old_terms, 0)
    for copy in stored(0):
        copy.wait()

    lane_r = lax.broadcasted_iota(jnp.int32, (ROWS, 128), 1)
    sub_r = lax.broadcasted_iota(jnp.int32, (ROWS, 128), 0)
    slope_z = (lane_r % KZ // 2 + c * (KZ // 2)).astype(f32) / KMAX

    def synth_y(h, xp):
        t = []
        for k in range(2):
            rows = pl.ds(2 * xp + k - 8 * h, ROWS, stride=8)
            tiles = [recv1[m, h, rows, :] for m in range(TILES)]
            sent = []
            for m in range(KY):
                tile, first = divmod(5 * KZ * m, 128)
                block = roll(tiles[tile], -first, 1)
                if first + 5 * KZ > 128:
                    block = jnp.where(lane_r < 128 - first, block, roll(tiles[tile + 1], -first, 1))
                sent.append(block)
            modes = []
            for m in range(KY):
                slope_y = (sub_r * (KY // 2) + m // 2).astype(f32) / KMAX
                dy = slope_y * (-sent[m - 1] if m % 2 else sent[m + 1])
                dz = slope_z * pair_swap(sent[m], 1)
                x_terms = roll(sent[m], KZ, 1)
                curl_x = roll(dy, KZ, 1) - roll(dz, 2 * KZ, 1)
                curl_y = roll(dz, 4 * KZ, 1) - x_terms
                curl_z = x_terms - roll(dy, 5 * KZ, 1)
                modes.append(
                    jnp.where(
                        lane_r < 3 * KZ,
                        sent[m],
                        jnp.where(lane_r < 4 * KZ, curl_x, jnp.where(lane_r < 5 * KZ, curl_y, curl_z)),
                    )
                )
            t.append(jnp.concatenate(modes, axis=0))
        high, low = split(jnp.concatenate(t, axis=1))
        rhs = jnp.concatenate([high, low, high, jnp.zeros((32, 256), bf16)], axis=0)
        o = dot(sy[...], rhs)
        send2[2 * xp] = o[:, :128]
        send2[2 * xp + 1] = o[:, 128:]

    for h in range(2):
        own1(h).wait()
        for i in range(1, ROWS):
            copy1(h, i).wait_recv()
        for g in range(h * CHUNKS // 2, (h + 1) * CHUNKS // 2):
            lax.fori_loop(g * XP, (g + 1) * XP, lambda xp, carry: (synth_y(h, xp), carry)[1], 0)
            own2(g).start()
            for i in range(1, COLS):
                copy2(g, i).start()

    lane_y = lax.broadcasted_iota(jnp.int32, (YL, 128), 1)

    def place(first):
        q = lane_y - first
        return jnp.where(q < 0, q + 128, q)

    def middle(xp, carry):
        sums = []
        for k in range(2):
            x = 2 * xp + k
            blocks = [roll(recv2[m, x], KZ * (m % 6), 1) for m in range(COLS)]
            tile1, tile2 = [], []
            for i in range(6):
                q = place(KZ * i)
                t = blocks[0]
                for m in range(1, 6):
                    t = jnp.where(q >= KZ * m, blocks[m], t)
                tile1.append(roll(t, -KZ * i, 1))
                tile2.append(roll(jnp.where(q >= KZ, blocks[7], blocks[6]), -KZ * i, 1))
            modes = jnp.concatenate([jnp.concatenate(tile1, axis=0), jnp.concatenate(tile2, axis=0)], axis=1)
            new = dot3(modes, szh, szl)
            u = [new[YL * i : YL * (i + 1)] for i in range(3)]
            w = [new[YL * i : YL * (i + 1)] for i in range(3, 6)]
            v0 = [vel[0, i, x] for i in range(3)]
            w0 = [vort[0, i, x] for i in range(3)]
            for i in range(3):
                a, b = (i + 1) % 3, (i + 2) % 3
                sums.append(part[i, x] + ((u[a] * w0[b] - u[b] * w0[a]) + (v0[a] * w[b] - v0[b] * w[a])))
        o = dot3(jnp.concatenate(sums, axis=0), zah, zal)
        out = [o[YL * j : YL * (j + 1)] for j in range(6)]
        for half in range(2):
            rolled = [roll(out[j][:, 128 * half : 128 * half + 128], OFFSETS[j], 1) for j in range(6)]
            for m in range(6 if half == 0 else 2):
                q = place(KZ * m)
                t = rolled[0]
                for j in range(1, 6):
                    t = jnp.where(q >= OFFSETS[j], rolled[j], t)
                send3[6 * half + m, xp] = roll(t, -KZ * m, 1)
        return carry

    for g in range(CHUNKS):
        own2(g).wait()
        for i in range(1, COLS):
            copy2(g, i).wait_recv()
        lax.fori_loop(g * XP, (g + 1) * XP, middle, 0)
        own3(g).start()
        for i in range(1, COLS):
            copy3(g, i).start()

    def analyze_y(h, xq):
        high, low = split(jnp.concatenate([recv3[2 * xq], recv3[2 * xq + 1]], axis=1))
        o = dot(ya[...], jnp.concatenate([high, low, high], axis=0))
        for k in range(2):
            for m in range(KY):
                rows = pl.ds(4 * (m % 2) + 2 * xq - 4 * h + k, ROWS, stride=8)
                send4[h, m // 2, rows, :] = o[ROWS * m : ROWS * (m + 1), 128 * k : 128 * k + 128]

    def analyze_x(h):
        rows = []
        for m in range(KY // 2):
            t = recv4[h, m].T
            rows.append(jnp.concatenate([t[0:64], t[64:128]], axis=1))
        high, low = split(jnp.concatenate(rows, axis=0))
        part_h, part_l = xah[256 * h : 256 * h + 256, :], xal[256 * h : 256 * h + 256, :]
        return dot(high, part_h) + (dot(low, part_h) + dot(high, part_l))

    for h in range(2):
        for g in range(h * CHUNKS // 2, (h + 1) * CHUNKS // 2):
            own3(g).wait()
            for i in range(1, COLS):
                copy3(g, i).wait_recv()
            for q in range(g * XP // 2, (g + 1) * XP // 2):
                analyze_y(h, q)
        own4(h).start()
        for i in range(1, ROWS):
            copy4(h, i).start()
    for h in range(2):
        own4(h).wait()
        for i in range(1, ROWS):
            copy4(h, i).wait_recv()
        if h == 0:
            fin[...] = analyze_x(0)
        else:
            fin[...] += analyze_x(1)

    def finish(pair, carry):
        first = 64 * pair
        s = [
            [fin[first + KZ * i : first + KZ * i + 24, 256 * k : 256 * k + 256] for i in range(3)] for k in range(2)
        ]
        wy = wave_y(pair)
        square = wy**2 + wave_z**2 + wave_x**2
        some = square > 0
        safe = jnp.where(some, square, 1.0)
        potential = []
        for k in range(2):
            wy_k = wy if k == 0 else -wy
            divergence = diff_x(s[k][0]) + wy_k * s[1 - k][1] + diff_z(s[k][2])
            potential.append(jnp.where(some, divergence / safe, 0.0))
        for k in range(2):
            wy_k = wy if k == 0 else -wy
            slopes = (diff_x(potential[k]), wy_k * potential[1 - k], diff_z(potential[k]))
            for i in range(3):
                out_ref[i, 2 * pair + k] = (s[k][i] + slopes[i])[0:KZ, 0:MODES]
        return carry

    for pair in range(KY // 2):
        finish(pair, 0)

    for h in range(2):
        for i in range(1, ROWS):
            copy1(h, i).wait_send()
            copy4(h, i).wait_send()
    for g in range(CHUNKS):
        for i in range(1, COLS):
            copy2(g, i).wait_send()
            copy3(g, i).wait_send()


def shards(new_velocity, stored_velocity, stored_vorticity):
    consts = tables()
    vmem = pl.BlockSpec(memory_space=pltpu.VMEM)
    hbm = pl.BlockSpec(memory_space=pltpu.HBM)
    dma = pltpu.SemaphoreType.DMA
    sums = pl.pallas_call(
        kernel,
        out_shape=jax.ShapeDtypeStruct((3, KY, KZ, MODES), f32),
        in_specs=[hbm, hbm, hbm] + [hbm] * TABLES,
        out_specs=vmem,
        scratch_shapes=[
            *(pltpu.VMEM(t.shape, bf16) for t in consts),
            pltpu.VMEM((3, KY, KZ, MODES), f32),
            pltpu.VMEM((3, 24, 256), f32),
            pltpu.VMEM((128 * TILES, 256), f32),
            pltpu.VMEM((ORDERS, 3, XL, YL, N), f32),
            pltpu.VMEM((ORDERS, 3, XL, YL, N), f32),
            pltpu.VMEM((3, XL, YL, N), f32),
            pltpu.VMEM((TILES, 2, 128, 128), f32),
            pltpu.VMEM((TILES, 2, 128, 128), f32),
            pltpu.VMEM((XL, N, 128), f32),
            pltpu.VMEM((COLS, XL, YL, 128), f32),
            pltpu.VMEM((COLS, XL // 2, YL, 128), f32),
            pltpu.VMEM((XL // 2, N, 128), f32),
            pltpu.VMEM((2, KY // 2, 128, 128), f32),
            pltpu.VMEM((2, KY // 2, 128, 128), f32),
            pltpu.VMEM((KY // 2 * 64, 512), f32),
            dma((2, ORDERS)),
            dma,
            dma((TABLES,)),
            dma((2, ROWS)),
            dma((2, ROWS)),
            dma((CHUNKS, COLS)),
            dma((CHUNKS, COLS)),
            dma((CHUNKS, COLS)),
            dma((CHUNKS, COLS)),
            dma((2, ROWS)),
            dma((2, ROWS)),
            dma((4 + 2 * CHUNKS,)),
        ],
        compiler_params=pltpu.CompilerParams(
            collective_id=0, has_side_effects=True, vmem_limit_bytes=46 * 2**20
        ),
        name="euler_order",
    )(*(pltpu.with_memory_space_constraint(x, pltpu.HBM) for x in (new_velocity, stored_velocity, stored_vorticity, *map(jnp.asarray, consts))))
    return sums / (ORDERS + 1)


def solution(mesh):
    return jax.shard_map(
        shards,
        mesh=mesh,
        in_specs=(
            P(None, "row", "col", None),
            P(None, None, "row", "col", None),
            P(None, None, "row", "col", None),
        ),
        out_specs=P(None, "row", "col", None),
        check_vma=False,
    )
```

```python
import jax
import jax.numpy as jnp
import numpy as np
from jax import lax
from jax.experimental import pallas as pl
from jax.experimental.pallas import tpu as pltpu
from jax.sharding import PartitionSpec as P

N = 256
MODES = 160
ORDERS = 6
KMAX = 79
ROWS, COLS = 16, 8
KY, KZ = MODES // ROWS, MODES // COLS
XL, YL = N // ROWS, N // COLS
CHUNKS = 4
XC = XL // CHUNKS
XP = XC // 2
OFFSETS = (0, 20, 40, 64, 84, 104)
TILES = 8
BLOCK1, BLOCK4 = 8 * TILES, 8 * (KY // 2)
TABLES = 10
MESH = pl.DeviceIdType.MESH
bf16, f32 = jnp.bfloat16, jnp.float32


def basis():
    p = np.arange(N)[:, None]
    m = np.arange(MODES)[None, :]
    k = m // 2
    angle = 2.0 * np.pi / N * (p * k % N)
    table = np.where(m % 2 == 0, np.cos(angle), np.sin(angle)) * np.sqrt(np.where(m < 2, 1.0, 2.0) / N)
    table[:, 1] = 0.0
    return table


def halves(table):
    high = np.asarray(table, jnp.bfloat16)
    low = np.asarray(table - high.astype(np.float64), jnp.bfloat16)
    return high, low


def tables():
    s = basis()
    sx = np.zeros((N, 256))
    sx[:, :MODES] = s.reshape(ROWS, 2, 8, MODES).transpose(1, 0, 2, 3).reshape(N, MODES)
    order = np.arange(MODES).reshape(ROWS, KY).T.reshape(-1)
    sy_h, sy_l = halves(s[:, order])
    sy = np.concatenate([sy_h, sy_h, sy_l, np.zeros((N, 32), jnp.bfloat16)], axis=1)
    sz = np.zeros((256, N))
    sz[:120] = s[:, :120].T
    sz[128:168] = s[:, 120:].T
    ya = np.concatenate([sy_h.T, sy_h.T, sy_l.T], axis=1)
    points = np.arange(N).reshape(ROWS, 2, 4, 2).transpose(1, 3, 0, 2)
    xa = np.zeros((2, 2, ROWS, 2, 4, 2, 256))
    for k in range(2):
        xa[:, :, :, k, :, k, :MODES] = s[points]
    xa = xa.reshape(512, 512)
    return (*halves(sx), sy, *halves(sz), *halves(sz.T), ya, *halves(xa))


def split(x):
    high = x.astype(bf16)
    return high, (x - high.astype(f32)).astype(bf16)


def dot(a, b):
    return jnp.dot(a, b, preferred_element_type=f32)


def dot_nt(a, b):
    return lax.dot_general(a, b, (((1,), (1,)), ((), ())), preferred_element_type=f32)


def dot3(x, table_h, table_l):
    high, low = split(x)
    return dot(high, table_h[...]) + (dot(low, table_h[...]) + dot(high, table_l[...]))


def roll(x, shift, axis):
    shift %= x.shape[axis]
    return x if shift == 0 else pltpu.roll(x, shift, axis)


def pair_swap(x, axis):
    even = lax.broadcasted_iota(jnp.int32, x.shape, axis) % 2 == 0
    return jnp.where(even, roll(x, -1, axis), -roll(x, 1, axis))


def kernel(
    a_hbm, vel_hbm, vort_hbm, *rest,
):
    tables_hbm, (out_ref, *tables_vmem), rest = rest[:TABLES], rest[TABLES : 2 * TABLES + 1], rest[2 * TABLES + 1 :]
    sxh, sxl, sy, szh, szl, zah, zal, ya, xah, xal = tables_vmem
    (
    a_ref, a_s, f_s, vel, vort, part, send1, recv1, send2, recv2, send3, recv3, send4, recv4, fin,
    hbm_sem, a_sem, table_sem, s1s, s1r, s2s, s2r, s3s, s3r, s4s, s4r, own,
    ) = rest
    r, c = lax.axis_index("row"), lax.axis_index("col")

    def row_peer(i):
        return lax.rem(r + i, ROWS)

    def col_peer(i):
        return lax.rem(c + i, COLS)

    def stored(o):
        return (
            pltpu.make_async_copy(vel_hbm.at[o], vel.at[o], hbm_sem.at[0, o]),
            pltpu.make_async_copy(vort_hbm.at[o], vort.at[o], hbm_sem.at[1, o]),
        )

    def table(i):
        return pltpu.make_async_copy(tables_hbm[i], tables_vmem[i], table_sem.at[i])

    first = pltpu.make_async_copy(a_hbm, a_ref, a_sem)
    first.start()
    table(0).start()
    table(1).start()

    barrier = pltpu.get_barrier_semaphore()
    for i in range(1, ROWS):
        pl.semaphore_signal(barrier, 1, device_id=(row_peer(i), c), device_id_type=MESH)
    for i in range(1, COLS):
        pl.semaphore_signal(barrier, 1, device_id=(r, col_peer(i)), device_id_type=MESH)

    def ds(start, size, unit):
        return pl.ds(pl.multiple_of(start, unit), size)

    def copy1(h, i):
        there = row_peer(i)
        return pltpu.make_async_remote_copy(
            send1.at[h, ds(there * BLOCK1, BLOCK1, 8), :],
            recv1.at[h, ds(r * BLOCK1, BLOCK1, 8), :],
            s1s.at[h], s1r.at[h], device_id=(there, c), device_id_type=MESH,
        )

    def copy2(g, i):
        there = col_peer(i)
        return pltpu.make_async_remote_copy(
            send2.at[pl.ds(g * XC, XC), ds(there * YL, YL, 8), :],
            recv2.at[c, pl.ds(g * XC, XC)],
            s2s.at[g], s2r.at[g], device_id=(r, there), device_id_type=MESH,
        )

    def copy3(g, i):
        there = col_peer(i)
        return pltpu.make_async_remote_copy(
            send3.at[there, pl.ds(g * XP, XP)],
            recv3.at[pl.ds(g * XP, XP), ds(c * YL, YL, 8), :],
            s3s.at[g], s3r.at[g], device_id=(r, there), device_id_type=MESH,
        )

    def copy4(h, i):
        there = row_peer(i)
        return pltpu.make_async_remote_copy(
            send4.at[h, ds(there * BLOCK4, BLOCK4, 8), :],
            recv4.at[h, ds(r * BLOCK4, BLOCK4, 8), :],
            s4s.at[h], s4r.at[h], device_id=(there, c), device_id_type=MESH,
        )

    def all_of(source, target, sent, arrived):
        return pltpu.make_async_remote_copy(
            source, target, sent, arrived, device_id=(row_peer(1), c), device_id_type=MESH
        )

    def all1(h):
        rows = pl.ds(0, (ROWS - 1) * BLOCK1)
        return all_of(send1.at[h, rows], recv1.at[h, rows], s1s.at[h], s1r.at[h])

    def all2(g):
        piece = pl.ds(g * XC, XC)
        return all_of(
            send2.at[piece, pl.ds(0, (COLS - 1) * YL)], recv2.at[pl.ds(0, COLS - 1), piece], s2s.at[g], s2r.at[g]
        )

    def all3(g):
        piece = pl.ds(g * XP, XP)
        return all_of(
            send3.at[pl.ds(0, COLS - 1), piece], recv3.at[piece, pl.ds(0, (COLS - 1) * YL)], s3s.at[g], s3r.at[g]
        )

    def all4(h):
        rows = pl.ds(0, (ROWS - 1) * BLOCK4)
        return all_of(send4.at[h, rows], recv4.at[h, rows], s4s.at[h], s4r.at[h])

    def own1(h):
        return pltpu.make_async_copy(
            send1.at[h, ds(r * BLOCK1, BLOCK1, 8), :], recv1.at[h, ds(r * BLOCK1, BLOCK1, 8), :], own.at[h]
        )

    def own4(h):
        return pltpu.make_async_copy(
            send4.at[h, ds(r * BLOCK4, BLOCK4, 8), :], recv4.at[h, ds(r * BLOCK4, BLOCK4, 8), :], own.at[2 + h]
        )

    def own2(g):
        return pltpu.make_async_copy(
            send2.at[pl.ds(g * XC, XC), ds(c * YL, YL, 8), :], recv2.at[c, pl.ds(g * XC, XC)], own.at[4 + g]
        )

    def own3(g):
        return pltpu.make_async_copy(
            send3.at[c, pl.ds(g * XP, XP)], recv3.at[pl.ds(g * XP, XP), ds(c * YL, YL, 8), :], own.at[4 + CHUNKS + g]
        )

    lane = lax.broadcasted_iota(jnp.int32, (24, 256), 1)
    sub = lax.broadcasted_iota(jnp.int32, (24, 256), 0)
    wave_x = (lane // 2).astype(f32) / KMAX
    wave_z = (sub // 2 + c * (KZ // 2)).astype(f32) / KMAX

    def wave_y(pair):
        return (jnp.zeros((24, 256), jnp.int32) + (r * (KY // 2) + pair)).astype(f32) / KMAX

    def diff_x(v):
        return wave_x * pair_swap(v, 1)

    def diff_z(v):
        return wave_z * pair_swap(v, 0)

    a_s[...] = jnp.zeros_like(a_s)
    f_s[...] = jnp.zeros_like(f_s)
    first.wait()
    for m in range(KY):
        for i in range(3):
            a_s[i, 0:KZ, 0:MODES] = a_ref[i, m]
        v = [a_s[i] for i in range(3)]
        v += [diff_x(v[2]), diff_x(v[1])]
        for i in range(5):
            first = KZ * (5 * m + i)
            f_s[first : first + KZ, :] = v[i][0:KZ]

    table(0).wait()
    table(1).wait()
    for i in range(2, TABLES):
        table(i).start()
    for o in (1, 5, 2, 4, 3, 0):
        for copy in stored(o):
            copy.start()
    for h in range(2):
        part_h, part_l = sxh[128 * h : 128 * h + 128, :], sxl[128 * h : 128 * h + 128, :]
        for t in range(TILES // 2):
            high, low = split(f_s[256 * t : 256 * t + 256, :])
            o = dot_nt(part_h, high) + (dot_nt(part_h, low) + dot_nt(part_l, high))
            for k in range(2):
                for there in range(ROWS):
                    first_row = BLOCK1 * there + 8 * (2 * t + k)
                    send1[h, first_row : first_row + 8, :] = o[8 * there : 8 * there + 8, 128 * k : 128 * k + 128]
        own1(h).start()
        if h == 0:
            pl.semaphore_wait(barrier, ROWS + COLS - 2)
        for i in range(1, ROWS):
            copy1(h, i).start()

    for i in range(2, TABLES):
        table(i).wait()
    for o in (1, 5, 2, 4, 3):
        for copy in stored(o):
            copy.wait()

    def old_terms(x, carry):
        acc = None
        for o in range(1, ORDERS):
            u = [vel[o, i, x] for i in range(3)]
            w = [vort[ORDERS - o, i, x] for i in range(3)]
            term = [u[1] * w[2] - u[2] * w[1], u[2] * w[0] - u[0] * w[2], u[0] * w[1] - u[1] * w[0]]
            acc = term if acc is None else [p + q for p, q in zip(acc, term)]
        for i in range(3):
            part[i, x] = acc[i]
        return carry

    lax.fori_loop(0, XL, old_terms, 0)
    for copy in stored(0):
        copy.wait()

    lane_r = lax.broadcasted_iota(jnp.int32, (ROWS, 128), 1)
    sub_r = lax.broadcasted_iota(jnp.int32, (ROWS, 128), 0)
    slope_z = (lane_r % KZ // 2 + c * (KZ // 2)).astype(f32) / KMAX

    def synth_y(h, xp):
        t = []
        for k in range(2):
            tiles = [recv1[h, pl.ds(8 * m + 2 * xp + k - 8 * h, ROWS, stride=BLOCK1), :] for m in range(TILES)]
            sent = []
            for m in range(KY):
                tile, first = divmod(5 * KZ * m, 128)
                block = roll(tiles[tile], -first, 1)
                if first + 5 * KZ > 128:
                    block = jnp.where(lane_r < 128 - first, block, roll(tiles[tile + 1], -first, 1))
                sent.append(block)
            modes = []
            for m in range(KY):
                slope_y = (sub_r * (KY // 2) + m // 2).astype(f32) / KMAX
                dy = slope_y * (-sent[m - 1] if m % 2 else sent[m + 1])
                dz = slope_z * pair_swap(sent[m], 1)
                x_terms = roll(sent[m], KZ, 1)
                curl_x = roll(dy, KZ, 1) - roll(dz, 2 * KZ, 1)
                curl_y = roll(dz, 4 * KZ, 1) - x_terms
                curl_z = x_terms - roll(dy, 5 * KZ, 1)
                modes.append(
                    jnp.where(
                        lane_r < 3 * KZ,
                        sent[m],
                        jnp.where(lane_r < 4 * KZ, curl_x, jnp.where(lane_r < 5 * KZ, curl_y, curl_z)),
                    )
                )
            t.append(jnp.concatenate(modes, axis=0))
        high, low = split(jnp.concatenate(t, axis=1))
        rhs = jnp.concatenate([high, low, high, jnp.zeros((32, 256), bf16)], axis=0)
        o = dot(sy[...], rhs)
        send2[2 * xp] = o[:, :128]
        send2[2 * xp + 1] = o[:, 128:]

    for h in range(2):
        own1(h).wait()
        all1(h).wait_recv()
        for g in range(h * CHUNKS // 2, (h + 1) * CHUNKS // 2):
            lax.fori_loop(g * XP, (g + 1) * XP, lambda xp, carry: (synth_y(h, xp), carry)[1], 0)
            own2(g).start()
            for i in range(1, COLS):
                copy2(g, i).start()

    lane_y = lax.broadcasted_iota(jnp.int32, (YL, 128), 1)

    def place(first):
        q = lane_y - first
        return jnp.where(q < 0, q + 128, q)

    def middle(xp, carry):
        sums = []
        for k in range(2):
            x = 2 * xp + k
            blocks = [roll(recv2[m, x], KZ * (m % 6), 1) for m in range(COLS)]
            tile1, tile2 = [], []
            for i in range(6):
                q = place(KZ * i)
                t = blocks[0]
                for m in range(1, 6):
                    t = jnp.where(q >= KZ * m, blocks[m], t)
                tile1.append(roll(t, -KZ * i, 1))
                tile2.append(roll(jnp.where(q >= KZ, blocks[7], blocks[6]), -KZ * i, 1))
            modes = jnp.concatenate([jnp.concatenate(tile1, axis=0), jnp.concatenate(tile2, axis=0)], axis=1)
            new = dot3(modes, szh, szl)
            u = [new[YL * i : YL * (i + 1)] for i in range(3)]
            w = [new[YL * i : YL * (i + 1)] for i in range(3, 6)]
            v0 = [vel[0, i, x] for i in range(3)]
            w0 = [vort[0, i, x] for i in range(3)]
            for i in range(3):
                a, b = (i + 1) % 3, (i + 2) % 3
                sums.append(part[i, x] + ((u[a] * w0[b] - u[b] * w0[a]) + (v0[a] * w[b] - v0[b] * w[a])))
        o = dot3(jnp.concatenate(sums, axis=0), zah, zal)
        out = [o[YL * j : YL * (j + 1)] for j in range(6)]
        for half in range(2):
            rolled = [roll(out[j][:, 128 * half : 128 * half + 128], OFFSETS[j], 1) for j in range(6)]
            for m in range(6 if half == 0 else 2):
                q = place(KZ * m)
                t = rolled[0]
                for j in range(1, 6):
                    t = jnp.where(q >= OFFSETS[j], rolled[j], t)
                send3[6 * half + m, xp] = roll(t, -KZ * m, 1)
        return carry

    for g in range(CHUNKS):
        own2(g).wait()
        all2(g).wait_recv()
        lax.fori_loop(g * XP, (g + 1) * XP, middle, 0)
        own3(g).start()
        for i in range(1, COLS):
            copy3(g, i).start()

    def analyze_y(h, xq):
        high, low = split(jnp.concatenate([recv3[2 * xq], recv3[2 * xq + 1]], axis=1))
        o = dot(ya[...], jnp.concatenate([high, low, high], axis=0))
        for k in range(2):
            for m in range(KY):
                rows = pl.ds(8 * (m // 2) + 4 * (m % 2) + 2 * xq - 4 * h + k, ROWS, stride=BLOCK4)
                send4[h, rows, :] = o[ROWS * m : ROWS * (m + 1), 128 * k : 128 * k + 128]

    def analyze_x(h):
        rows = []
        for m in range(KY // 2):
            firsts = [BLOCK4 * there + 8 * m for there in range(ROWS)]
            t = jnp.concatenate([recv4[h, first_row : first_row + 8, :] for first_row in firsts], axis=0).T
            rows.append(jnp.concatenate([t[0:64], t[64:128]], axis=1))
        high, low = split(jnp.concatenate(rows, axis=0))
        part_h, part_l = xah[256 * h : 256 * h + 256, :], xal[256 * h : 256 * h + 256, :]
        return dot(high, part_h) + (dot(low, part_h) + dot(high, part_l))

    for h in range(2):
        for g in range(h * CHUNKS // 2, (h + 1) * CHUNKS // 2):
            own3(g).wait()
            all3(g).wait_recv()
            for q in range(g * XP // 2, (g + 1) * XP // 2):
                analyze_y(h, q)
        own4(h).start()
        for i in range(1, ROWS):
            copy4(h, i).start()
    for h in range(2):
        all1(h).wait_send()
    for g in range(CHUNKS):
        all2(g).wait_send()
        all3(g).wait_send()
    for h in range(2):
        own4(h).wait()
        all4(h).wait_send()
        all4(h).wait_recv()
        if h == 0:
            fin[...] = analyze_x(0)
        else:
            fin[...] += analyze_x(1)

    def finish(pair, carry):
        first = 64 * pair
        s = [
            [fin[first + KZ * i : first + KZ * i + 24, 256 * k : 256 * k + 256] for i in range(3)] for k in range(2)
        ]
        wy = wave_y(pair)
        square = wy**2 + wave_z**2 + wave_x**2
        some = square > 0
        safe = jnp.where(some, square, 1.0)
        potential = []
        for k in range(2):
            wy_k = wy if k == 0 else -wy
            divergence = diff_x(s[k][0]) + wy_k * s[1 - k][1] + diff_z(s[k][2])
            potential.append(jnp.where(some, divergence / safe, 0.0))
        for k in range(2):
            wy_k = wy if k == 0 else -wy
            slopes = (diff_x(potential[k]), wy_k * potential[1 - k], diff_z(potential[k]))
            for i in range(3):
                out_ref[i, 2 * pair + k] = (s[k][i] + slopes[i])[0:KZ, 0:MODES]
        return carry

    for pair in range(KY // 2):
        finish(pair, 0)


def shards(new_velocity, stored_velocity, stored_vorticity):
    consts = tables()
    vmem = pl.BlockSpec(memory_space=pltpu.VMEM)
    hbm = pl.BlockSpec(memory_space=pltpu.HBM)
    dma = pltpu.SemaphoreType.DMA
    sums = pl.pallas_call(
        kernel,
        out_shape=jax.ShapeDtypeStruct((3, KY, KZ, MODES), f32),
        in_specs=[hbm, hbm, hbm] + [hbm] * TABLES,
        out_specs=vmem,
        scratch_shapes=[
            *(pltpu.VMEM(t.shape, bf16) for t in consts),
            pltpu.VMEM((3, KY, KZ, MODES), f32),
            pltpu.VMEM((3, 24, 256), f32),
            pltpu.VMEM((128 * TILES, 256), f32),
            pltpu.VMEM((ORDERS, 3, XL, YL, N), f32),
            pltpu.VMEM((ORDERS, 3, XL, YL, N), f32),
            pltpu.VMEM((3, XL, YL, N), f32),
            pltpu.VMEM((2, ROWS * BLOCK1, 128), f32),
            pltpu.VMEM((2, ROWS * BLOCK1, 128), f32),
            pltpu.VMEM((XL, N, 128), f32),
            pltpu.VMEM((COLS, XL, YL, 128), f32),
            pltpu.VMEM((COLS, XL // 2, YL, 128), f32),
            pltpu.VMEM((XL // 2, N, 128), f32),
            pltpu.VMEM((2, ROWS * BLOCK4, 128), f32),
            pltpu.VMEM((2, ROWS * BLOCK4, 128), f32),
            pltpu.VMEM((KY // 2 * 64, 512), f32),
            dma((2, ORDERS)),
            dma,
            dma((TABLES,)),
            dma((2,)),
            dma((2,)),
            dma((CHUNKS,)),
            dma((CHUNKS,)),
            dma((CHUNKS,)),
            dma((CHUNKS,)),
            dma((2,)),
            dma((2,)),
            dma((4 + 2 * CHUNKS,)),
        ],
        compiler_params=pltpu.CompilerParams(
            collective_id=0, has_side_effects=True, vmem_limit_bytes=46 * 2**20
        ),
        name="euler_order",
    )(*(pltpu.with_memory_space_constraint(x, pltpu.HBM) for x in (new_velocity, stored_velocity, stored_vorticity, *map(jnp.asarray, consts))))
    return sums / (ORDERS + 1)


def solution(mesh):
    return jax.shard_map(
        shards,
        mesh=mesh,
        in_specs=(
            P(None, "row", "col", None),
            P(None, None, "row", "col", None),
            P(None, None, "row", "col", None),
        ),
        out_specs=P(None, "row", "col", None),
        check_vma=False,
    )
```

```python
import jax
import jax.numpy as jnp
import numpy as np
from jax import lax
from jax.experimental import pallas as pl
from jax.experimental.pallas import tpu as pltpu
from jax.sharding import PartitionSpec as P

N = 256
MODES = 160
ORDERS = 6
KMAX = 79
ROWS, COLS = 16, 8
KY, KZ = MODES // ROWS, MODES // COLS
XL, YL = N // ROWS, N // COLS
CHUNKS = 4
XC = XL // CHUNKS
XP = XC // 2
OFFSETS = (0, 20, 40, 64, 84, 104)
TILES = 8
BLOCK1, BLOCK4 = 8 * TILES, 8 * (KY // 2)
TABLES = 10
MESH = pl.DeviceIdType.MESH
bf16, f32 = jnp.bfloat16, jnp.float32


def basis():
    p = np.arange(N)[:, None]
    m = np.arange(MODES)[None, :]
    k = m // 2
    angle = 2.0 * np.pi / N * (p * k % N)
    table = np.where(m % 2 == 0, np.cos(angle), np.sin(angle)) * np.sqrt(np.where(m < 2, 1.0, 2.0) / N)
    table[:, 1] = 0.0
    return table


def halves(table):
    high = np.asarray(table, jnp.bfloat16)
    low = np.asarray(table - high.astype(np.float64), jnp.bfloat16)
    return high, low


def tables():
    s = basis()
    sx = np.zeros((N, 256))
    sx[:, :MODES] = s.reshape(ROWS, 2, 8, MODES).transpose(1, 0, 2, 3).reshape(N, MODES)
    order = np.arange(MODES).reshape(ROWS, KY).T.reshape(-1)
    sy_h, sy_l = halves(s[:, order])
    sy = np.concatenate([sy_h, sy_h, sy_l, np.zeros((N, 32), jnp.bfloat16)], axis=1)
    sz = np.zeros((256, N))
    sz[:120] = s[:, :120].T
    sz[128:168] = s[:, 120:].T
    ya = np.concatenate([sy_h.T, sy_h.T, sy_l.T], axis=1)
    points = np.arange(N).reshape(ROWS, 2, 4, 2).transpose(1, 3, 0, 2)
    xa = np.zeros((2, 2, ROWS, 2, 4, 2, 256))
    for k in range(2):
        xa[:, :, :, k, :, k, :MODES] = s[points]
    xa = xa.reshape(512, 512)
    return (*halves(sx), sy, *halves(sz), *halves(sz.T), ya, *halves(xa))


def split(x):
    high = x.astype(bf16)
    return high, (x - high.astype(f32)).astype(bf16)


def dot(a, b):
    return jnp.dot(a, b, preferred_element_type=f32)


def dot_nt(a, b):
    return lax.dot_general(a, b, (((1,), (1,)), ((), ())), preferred_element_type=f32)


def dot3(x, table_h, table_l):
    high, low = split(x)
    return dot(high, table_h[...]) + (dot(low, table_h[...]) + dot(high, table_l[...]))


def roll(x, shift, axis):
    shift %= x.shape[axis]
    return x if shift == 0 else pltpu.roll(x, shift, axis)


def pair_swap(x, axis):
    even = lax.broadcasted_iota(jnp.int32, x.shape, axis) % 2 == 0
    return jnp.where(even, roll(x, -1, axis), -roll(x, 1, axis))


def kernel(
    a_hbm, vel_hbm, vort_hbm, *rest,
):
    tables_hbm, (out_ref, *tables_vmem), rest = rest[:TABLES], rest[TABLES : 2 * TABLES + 1], rest[2 * TABLES + 1 :]
    sxh, sxl, sy, szh, szl, zah, zal, ya, xah, xal = tables_vmem
    (
    a_ref, a_s, f_s, vel, vort, part, send1, recv1, send2, recv2, send3, recv3, send4, recv4, fin,
    hbm_sem, a_sem, table_sem, s1s, s1r, s2s, s2r, s3s, s3r, s4s, s4r, own,
    ) = rest
    r, c = lax.axis_index("row"), lax.axis_index("col")

    def row_peer(i):
        return lax.rem(r + i, ROWS)

    def col_peer(i):
        return lax.rem(c + i, COLS)

    def stored(o):
        return (
            pltpu.make_async_copy(vel_hbm.at[o], vel.at[o], hbm_sem.at[0, o]),
            pltpu.make_async_copy(vort_hbm.at[o], vort.at[o], hbm_sem.at[1, o]),
        )

    def table(i):
        return pltpu.make_async_copy(tables_hbm[i], tables_vmem[i], table_sem.at[i])

    first = pltpu.make_async_copy(a_hbm, a_ref, a_sem)
    first.start()
    table(0).start()
    table(1).start()

    barrier = pltpu.get_barrier_semaphore()
    for i in range(1, ROWS):
        pl.semaphore_signal(barrier, 1, device_id=(row_peer(i), c), device_id_type=MESH)
    for i in range(1, COLS):
        pl.semaphore_signal(barrier, 1, device_id=(r, col_peer(i)), device_id_type=MESH)

    def ds(start, size, unit):
        return pl.ds(pl.multiple_of(start, unit), size)

    def copy1(h, i):
        there = row_peer(i)
        return pltpu.make_async_remote_copy(
            send1.at[h, ds(there * BLOCK1, BLOCK1, 8), :],
            recv1.at[h, ds(r * BLOCK1, BLOCK1, 8), :],
            s1s.at[h], s1r.at[h], device_id=(there, c), device_id_type=MESH,
        )

    def copy2(g, i):
        there = col_peer(i)
        return pltpu.make_async_remote_copy(
            send2.at[pl.ds(g * XC, XC), ds(there * YL, YL, 8), :],
            recv2.at[c, pl.ds(g * XC, XC)],
            s2s.at[g], s2r.at[g], device_id=(r, there), device_id_type=MESH,
        )

    def copy3(g, i):
        there = col_peer(i)
        return pltpu.make_async_remote_copy(
            send3.at[there, pl.ds(g * XP, XP)],
            recv3.at[pl.ds(g * XP, XP), ds(c * YL, YL, 8), :],
            s3s.at[g], s3r.at[g], device_id=(r, there), device_id_type=MESH,
        )

    def copy4(h, i):
        there = row_peer(i)
        return pltpu.make_async_remote_copy(
            send4.at[h, ds(there * BLOCK4, BLOCK4, 8), :],
            recv4.at[h, ds(r * BLOCK4, BLOCK4, 8), :],
            s4s.at[h], s4r.at[h], device_id=(there, c), device_id_type=MESH,
        )

    def all_of(source, target, sent, arrived):
        return pltpu.make_async_remote_copy(
            source, target, sent, arrived, device_id=(row_peer(1), c), device_id_type=MESH
        )

    def all1(h):
        rows = pl.ds(0, (ROWS - 1) * BLOCK1)
        return all_of(send1.at[h, rows], recv1.at[h, rows], s1s.at[h], s1r.at[h])

    def all2(g):
        piece = pl.ds(g * XC, XC)
        return all_of(
            send2.at[piece, pl.ds(0, (COLS - 1) * YL)], recv2.at[pl.ds(0, COLS - 1), piece], s2s.at[g], s2r.at[g]
        )

    def all3(g):
        piece = pl.ds(g * XP, XP)
        return all_of(
            send3.at[pl.ds(0, COLS - 1), piece], recv3.at[piece, pl.ds(0, (COLS - 1) * YL)], s3s.at[g], s3r.at[g]
        )

    def all4(h):
        rows = pl.ds(0, (ROWS - 1) * BLOCK4)
        return all_of(send4.at[h, rows], recv4.at[h, rows], s4s.at[h], s4r.at[h])

    def own1(h):
        return pltpu.make_async_copy(
            send1.at[h, ds(r * BLOCK1, BLOCK1, 8), :], recv1.at[h, ds(r * BLOCK1, BLOCK1, 8), :], own.at[h]
        )

    def own4(h):
        return pltpu.make_async_copy(
            send4.at[h, ds(r * BLOCK4, BLOCK4, 8), :], recv4.at[h, ds(r * BLOCK4, BLOCK4, 8), :], own.at[2 + h]
        )

    def own2(g):
        return pltpu.make_async_copy(
            send2.at[pl.ds(g * XC, XC), ds(c * YL, YL, 8), :], recv2.at[c, pl.ds(g * XC, XC)], own.at[4 + g]
        )

    def own3(g):
        return pltpu.make_async_copy(
            send3.at[c, pl.ds(g * XP, XP)], recv3.at[pl.ds(g * XP, XP), ds(c * YL, YL, 8), :], own.at[4 + CHUNKS + g]
        )

    lane = lax.broadcasted_iota(jnp.int32, (24, 256), 1)
    sub = lax.broadcasted_iota(jnp.int32, (24, 256), 0)
    wave_x = (lane // 2).astype(f32) / KMAX
    wave_z = (sub // 2 + c * (KZ // 2)).astype(f32) / KMAX

    def wave_y(pair):
        return (jnp.zeros((24, 256), jnp.int32) + (r * (KY // 2) + pair)).astype(f32) / KMAX

    def diff_x(v):
        return wave_x * pair_swap(v, 1)

    def diff_z(v):
        return wave_z * pair_swap(v, 0)

    a_s[...] = jnp.zeros_like(a_s)
    f_s[5 * KY * KZ :, :] = jnp.zeros((128 * TILES - 5 * KY * KZ, 256), f32)
    first.wait()
    for m in range(KY):
        for i in range(3):
            a_s[i, 0:KZ, 0:MODES] = a_ref[i, m]
        v = [a_s[i] for i in range(3)]
        v += [diff_x(v[2]), diff_x(v[1])]
        for i in range(5):
            first = KZ * (5 * m + i)
            f_s[first : first + KZ, :] = v[i][0:KZ]

    table(0).wait()
    table(1).wait()
    for i in range(2, TABLES):
        table(i).start()
    for o in (1, 5, 2, 4, 3, 0):
        for copy in stored(o):
            copy.start()
    for h in range(2):
        part_h, part_l = sxh[128 * h : 128 * h + 128, :], sxl[128 * h : 128 * h + 128, :]
        for t in range(TILES // 2):
            high, low = split(f_s[256 * t : 256 * t + 256, :])
            o = dot_nt(part_h, high) + (dot_nt(part_h, low) + dot_nt(part_l, high))
            for k in range(2):
                for there in range(ROWS):
                    first_row = BLOCK1 * there + 8 * (2 * t + k)
                    send1[h, first_row : first_row + 8, :] = o[8 * there : 8 * there + 8, 128 * k : 128 * k + 128]
        own1(h).start()
        if h == 0:
            pl.semaphore_wait(barrier, ROWS + COLS - 2)
        for i in range(1, ROWS):
            copy1(h, i).start()

    for i in range(2, TABLES):
        table(i).wait()
    for o in (1, 5, 2, 4, 3):
        for copy in stored(o):
            copy.wait()

    def old_terms(x, carry):
        acc = None
        for o in range(1, ORDERS):
            u = [vel[o, i, x] for i in range(3)]
            w = [vort[ORDERS - o, i, x] for i in range(3)]
            term = [u[1] * w[2] - u[2] * w[1], u[2] * w[0] - u[0] * w[2], u[0] * w[1] - u[1] * w[0]]
            acc = term if acc is None else [p + q for p, q in zip(acc, term)]
        for i in range(3):
            part[i, x] = acc[i]
        return carry

    lax.fori_loop(0, XL, old_terms, 0)
    for copy in stored(0):
        copy.wait()

    lane_r = lax.broadcasted_iota(jnp.int32, (ROWS, 128), 1)
    sub_r = lax.broadcasted_iota(jnp.int32, (ROWS, 128), 0)
    slope_z = (lane_r % KZ // 2 + c * (KZ // 2)).astype(f32) / KMAX

    def synth_y(h, xp):
        t = []
        for k in range(2):
            tiles = [recv1[h, pl.ds(8 * m + 2 * xp + k - 8 * h, ROWS, stride=BLOCK1), :] for m in range(TILES)]
            sent = []
            for m in range(KY):
                tile, first = divmod(5 * KZ * m, 128)
                block = roll(tiles[tile], -first, 1)
                if first + 5 * KZ > 128:
                    block = jnp.where(lane_r < 128 - first, block, roll(tiles[tile + 1], -first, 1))
                sent.append(block)
            modes = []
            for m in range(KY):
                slope_y = (sub_r * (KY // 2) + m // 2).astype(f32) / KMAX
                dy = slope_y * (-sent[m - 1] if m % 2 else sent[m + 1])
                dz = slope_z * pair_swap(sent[m], 1)
                x_terms = roll(sent[m], KZ, 1)
                curl_x = roll(dy, KZ, 1) - roll(dz, 2 * KZ, 1)
                curl_y = roll(dz, 4 * KZ, 1) - x_terms
                curl_z = x_terms - roll(dy, 5 * KZ, 1)
                modes.append(
                    jnp.where(
                        lane_r < 3 * KZ,
                        sent[m],
                        jnp.where(lane_r < 4 * KZ, curl_x, jnp.where(lane_r < 5 * KZ, curl_y, curl_z)),
                    )
                )
            t.append(jnp.concatenate(modes, axis=0))
        high, low = split(jnp.concatenate(t, axis=1))
        rhs = jnp.concatenate([high, low, high, jnp.zeros((32, 256), bf16)], axis=0)
        o = dot(sy[...], rhs)
        send2[2 * xp] = o[:, :128]
        send2[2 * xp + 1] = o[:, 128:]

    for h in range(2):
        own1(h).wait()
        all1(h).wait_recv()
        for g in range(h * CHUNKS // 2, (h + 1) * CHUNKS // 2):
            lax.fori_loop(g * XP, (g + 1) * XP, lambda xp, carry: (synth_y(h, xp), carry)[1], 0)
            for i in range(1, COLS):
                copy2(g, i).start()
            own2(g).start()

    lane_y = lax.broadcasted_iota(jnp.int32, (YL, 128), 1)

    def place(first):
        q = lane_y - first
        return jnp.where(q < 0, q + 128, q)

    def middle(xp, carry):
        sums = []
        for k in range(2):
            x = 2 * xp + k
            blocks = [roll(recv2[m, x], KZ * (m % 6), 1) for m in range(COLS)]
            tile1, tile2 = [], []
            for i in range(6):
                q = place(KZ * i)
                t = blocks[0]
                for m in range(1, 6):
                    t = jnp.where(q >= KZ * m, blocks[m], t)
                tile1.append(roll(t, -KZ * i, 1))
                tile2.append(roll(jnp.where(q >= KZ, blocks[7], blocks[6]), -KZ * i, 1))
            modes = jnp.concatenate([jnp.concatenate(tile1, axis=0), jnp.concatenate(tile2, axis=0)], axis=1)
            new = dot3(modes, szh, szl)
            u = [new[YL * i : YL * (i + 1)] for i in range(3)]
            w = [new[YL * i : YL * (i + 1)] for i in range(3, 6)]
            v0 = [vel[0, i, x] for i in range(3)]
            w0 = [vort[0, i, x] for i in range(3)]
            for i in range(3):
                a, b = (i + 1) % 3, (i + 2) % 3
                sums.append(part[i, x] + ((u[a] * w0[b] - u[b] * w0[a]) + (v0[a] * w[b] - v0[b] * w[a])))
        o = dot3(jnp.concatenate(sums, axis=0), zah, zal)
        out = [o[YL * j : YL * (j + 1)] for j in range(6)]
        for half in range(2):
            rolled = [roll(out[j][:, 128 * half : 128 * half + 128], OFFSETS[j], 1) for j in range(6)]
            for m in range(6 if half == 0 else 2):
                q = place(KZ * m)
                t = rolled[0]
                for j in range(1, 6):
                    t = jnp.where(q >= OFFSETS[j], rolled[j], t)
                send3[6 * half + m, xp] = roll(t, -KZ * m, 1)
        return carry

    for g in range(CHUNKS):
        own2(g).wait()
        all2(g).wait_recv()
        lax.fori_loop(g * XP, (g + 1) * XP, middle, 0)
        for i in range(1, COLS):
            copy3(g, i).start()
        own3(g).start()

    def analyze_y(h, xq):
        high, low = split(jnp.concatenate([recv3[2 * xq], recv3[2 * xq + 1]], axis=1))
        o = dot(ya[...], jnp.concatenate([high, low, high], axis=0))
        for k in range(2):
            for m in range(KY):
                rows = pl.ds(8 * (m // 2) + 4 * (m % 2) + 2 * xq - 4 * h + k, ROWS, stride=BLOCK4)
                send4[h, rows, :] = o[ROWS * m : ROWS * (m + 1), 128 * k : 128 * k + 128]

    def analyze_x(h):
        rows = []
        for m in range(KY // 2):
            firsts = [BLOCK4 * there + 8 * m for there in range(ROWS)]
            t = jnp.concatenate([recv4[h, first_row : first_row + 8, :] for first_row in firsts], axis=0).T
            rows.append(jnp.concatenate([t[0:64], t[64:128]], axis=1))
        high, low = split(jnp.concatenate(rows, axis=0))
        part_h, part_l = xah[256 * h : 256 * h + 256, :], xal[256 * h : 256 * h + 256, :]
        return dot(high, part_h) + (dot(low, part_h) + dot(high, part_l))

    for h in range(2):
        for g in range(h * CHUNKS // 2, (h + 1) * CHUNKS // 2):
            own3(g).wait()
            all3(g).wait_recv()
            for q in range(g * XP // 2, (g + 1) * XP // 2):
                analyze_y(h, q)
        for i in range(1, ROWS):
            copy4(h, i).start()
        own4(h).start()
    for h in range(2):
        all1(h).wait_send()
    for g in range(CHUNKS):
        all2(g).wait_send()
        all3(g).wait_send()
    for h in range(2):
        own4(h).wait()
        all4(h).wait_send()
        all4(h).wait_recv()
        if h == 0:
            fin[...] = analyze_x(0)
        else:
            fin[...] += analyze_x(1)

    def finish(pair, carry):
        first = 64 * pair
        s = [
            [fin[first + KZ * i : first + KZ * i + 24, 256 * k : 256 * k + 256] for i in range(3)] for k in range(2)
        ]
        wy = wave_y(pair)
        square = wy**2 + wave_z**2 + wave_x**2
        some = square > 0
        safe = jnp.where(some, square, 1.0)
        potential = []
        for k in range(2):
            wy_k = wy if k == 0 else -wy
            divergence = diff_x(s[k][0]) + wy_k * s[1 - k][1] + diff_z(s[k][2])
            potential.append(jnp.where(some, divergence / safe, 0.0))
        for k in range(2):
            wy_k = wy if k == 0 else -wy
            slopes = (diff_x(potential[k]), wy_k * potential[1 - k], diff_z(potential[k]))
            for i in range(3):
                out_ref[i, 2 * pair + k] = (s[k][i] + slopes[i])[0:KZ, 0:MODES]
        return carry

    for pair in range(KY // 2):
        finish(pair, 0)


def shards(new_velocity, stored_velocity, stored_vorticity):
    consts = tables()
    vmem = pl.BlockSpec(memory_space=pltpu.VMEM)
    hbm = pl.BlockSpec(memory_space=pltpu.HBM)
    dma = pltpu.SemaphoreType.DMA
    sums = pl.pallas_call(
        kernel,
        out_shape=jax.ShapeDtypeStruct((3, KY, KZ, MODES), f32),
        in_specs=[hbm, hbm, hbm] + [hbm] * TABLES,
        out_specs=vmem,
        scratch_shapes=[
            *(pltpu.VMEM(t.shape, bf16) for t in consts),
            pltpu.VMEM((3, KY, KZ, MODES), f32),
            pltpu.VMEM((3, 24, 256), f32),
            pltpu.VMEM((128 * TILES, 256), f32),
            pltpu.VMEM((ORDERS, 3, XL, YL, N), f32),
            pltpu.VMEM((ORDERS, 3, XL, YL, N), f32),
            pltpu.VMEM((3, XL, YL, N), f32),
            pltpu.VMEM((2, ROWS * BLOCK1, 128), f32),
            pltpu.VMEM((2, ROWS * BLOCK1, 128), f32),
            pltpu.VMEM((XL, N, 128), f32),
            pltpu.VMEM((COLS, XL, YL, 128), f32),
            pltpu.VMEM((COLS, XL // 2, YL, 128), f32),
            pltpu.VMEM((XL // 2, N, 128), f32),
            pltpu.VMEM((2, ROWS * BLOCK4, 128), f32),
            pltpu.VMEM((2, ROWS * BLOCK4, 128), f32),
            pltpu.VMEM((KY // 2 * 64, 512), f32),
            dma((2, ORDERS)),
            dma,
            dma((TABLES,)),
            dma((2,)),
            dma((2,)),
            dma((CHUNKS,)),
            dma((CHUNKS,)),
            dma((CHUNKS,)),
            dma((CHUNKS,)),
            dma((2,)),
            dma((2,)),
            dma((4 + 2 * CHUNKS,)),
        ],
        compiler_params=pltpu.CompilerParams(
            collective_id=0, has_side_effects=True, vmem_limit_bytes=46 * 2**20
        ),
        name="euler_order",
    )(*(pltpu.with_memory_space_constraint(x, pltpu.HBM) for x in (new_velocity, stored_velocity, stored_vorticity, *map(jnp.asarray, consts))))
    return sums / (ORDERS + 1)


def solution(mesh):
    return jax.shard_map(
        shards,
        mesh=mesh,
        in_specs=(
            P(None, "row", "col", None),
            P(None, None, "row", "col", None),
            P(None, None, "row", "col", None),
        ),
        out_specs=P(None, "row", "col", None),
        check_vma=False,
    )
```
